32 devices in a mesh: groups: 1, expert: 16 (over z, y, core), tensor: 2 (over x).
Axes of the slice: x: 2, y: 2, z: 4, core: 2. Of those that a mesh axis runs over, the one named last changes fastest.
Arguments:
- tokens: bfloat16 [2048, 4096], P(('groups', 'expert')), may hold values from -6 to 6
- expert_ids: int32 [2048, 8], P(('groups', 'expert')), may hold values from 0 to 15, all different within a row; in each aligned block of 128 rows (0 to 127, 128 to 255, ...) at most 96 rows name the same one
- route_weights: float32 [2048, 8], P(('groups', 'expert')), may hold values from 0.1 to 1
- gate_w: bfloat16 [16, 4096, 1536], P('expert', None, 'tensor'), may hold values from -0.09375 to 0.09375
- up_w: bfloat16 [16, 4096, 1536], P('expert', None, 'tensor'), may hold values from -0.09375 to 0.09375
- down_w: bfloat16 [16, 1536, 4096], P('expert', 'tensor'), may hold values from -0.15625 to 0.15625
Outputs:
- moe_out: bfloat16 [2048, 4096], P(('groups', 'expert'), 'tensor')
The draws below stay inside these ranges and needn't reach their ends.
Inputs may be any that keep to these rules, and one draw needn't show every extreme that they name: `expert_ids`: each row names 8 different experts. Among the rows of one device (aligned blocks of 128 rows) no expert is named more than 96 times, a bound that some block reaches.
All inputs are finite; a program needn't handle non-finite values.
Results may differ from the reference program's by a relative error of at most 0.014.
Values may be sent and summed in bfloat16 or wider, within the bound.
A program may use at most 128 MiB of HBM per device.

```python
import math
import jax
import jax.numpy as jnp
import numpy as np
from jax import lax

D = 4096
FF = 1536
TOK_DEV = 128
EXPERTS = 16
TOP = 8
CAP = 96
TOKENS = 2048


def block_levels(rng, extent, pieces, least, high):
    loudness, own = 1.0, jax.random.fold_in(rng, 6)
    for dim, shards_of in pieces:
        steps = jnp.exp(jax.random.uniform(jax.random.fold_in(own, dim), (shards_of,), jnp.float32, least / len(pieces), high / len(pieces)))
        loudness = loudness * jnp.repeat(steps, extent[dim] // shards_of).reshape([-1 if axis == dim else 1 for axis in range(len(extent))])
    return loudness


def routed_block(stream_key, own, number, rows, number_of, top, reach, slope):
    order = jax.random.permutation(stream_key, number_of)
    crowded, common = portions_of(number_of, rows * top, reach, slope, True), portions_of(number_of, rows * top, reach, slope, False)
    places = jnp.arange(number_of)

    def named(tallies, turn):
        used = int((tallies > 0).sum())
        fixed = max(1, used // 4)
        passed = fixed + (places - fixed + turn * (used - fixed)) % max(1, number_of - fixed)
        return jnp.zeros((number_of,), jnp.int32).at[order[jnp.where(places < fixed, places, passed)]].set(jnp.asarray(tallies, jnp.int32))

    tallies = jnp.where(number % 4 == 0, named(crowded, number // 4), named(common, number - number // 4 - 1))
    mixed = jax.random.permutation(jax.random.fold_in(own, 3), number_of)
    donor, sink = mixed[0:number_of // 2 * 2:2], mixed[1:number_of // 2 * 2:2]
    margin = jnp.minimum(tallies[donor] - 1, reach - tallies[sink]) // 2
    margin = jnp.where((donor == order[0]) | (sink == order[0]) | (tallies[sink] == 0), 0, jnp.maximum(margin, 0))
    passed = jax.random.randint(jax.random.fold_in(own, 4), (number_of // 2,), 0, 1 << 20) % (margin + 1)
    tallies = tallies.at[donor].add(-passed).at[sink].add(passed)
    members = jnp.searchsorted(jnp.cumsum(tallies), jnp.arange(rows * top), side="right").astype(jnp.int32)
    listing = members.reshape(top, rows).T
    listing = listing[jax.random.permutation(jax.random.fold_in(own, 1), rows)]
    turn = jax.random.randint(jax.random.fold_in(own, 2), (rows, 1), 0, top)
    return jnp.take_along_axis(listing, (jnp.arange(top)[None, :] + turn) % top, axis=1)


def portions_of(number_of, total, bound, slope, full):
    weights = [(1 << 20) // math.isqrt(grade ** slope) + 1 for grade in range(1, number_of + 1)]
    largest = bound if full else min(bound, max(-(-total // number_of), total * weights[0] // sum(weights)))
    least = 1 if total - largest >= number_of - 1 else 0
    holding, rest = [largest] + [least] * (number_of - 1), total - largest - least * (number_of - 1)
    while rest > 0:
        movable = [i for i in range(1, number_of) if holding[i] < largest] or [i for i in range(1, number_of) if holding[i] < bound]
        pool, remaining = sum([weights[i] for i in movable]), rest
        for i in movable:
            more = min(bound - holding[i], max(1, remaining * weights[i] // pool), rest)
            holding[i] = holding[i] + more
            rest = rest - more
    return np.array(holding)


def normal_values(stream_key, shape, spread, most, shards=(), kind=jnp.bfloat16):
    values = spread * jax.random.normal(stream_key, shape, jnp.float32)
    if shards:
        values = values * block_levels(stream_key, shape, shards, -0.22, 0.18)
    return jnp.clip(values, -most, most).astype(kind)


def setup_inputs(seed: int = 0, part: int = 0) -> dict:
    splits = jax.random.split(jax.random.key(seed), 7)
    own_keys = jax.random.split(jax.random.fold_in(splits[6], part), 7)
    tokens = normal_values(own_keys[0], (TOKENS, D), 1.0, 6.0, ((0, 16),))
    expert_ids_keys = jax.random.split(jax.random.fold_in(own_keys[1], 1), TOKENS // TOK_DEV)
    expert_ids_turns = jax.random.permutation(jax.random.fold_in(own_keys[1], 3), TOKENS // TOK_DEV)
    expert_ids = jax.vmap(lambda own, number: routed_block(jax.random.fold_in(own_keys[1], 2), own, number, TOK_DEV, EXPERTS, TOP, CAP, 2))(expert_ids_keys, expert_ids_turns).reshape((TOKENS, TOP))
    route_weights = jnp.clip(0.1 + 0.9 * jax.random.uniform(own_keys[2], (TOKENS, TOP), jnp.float32) ** block_levels(own_keys[2], (TOKENS, TOP), ((0, 16),), -0.2, 0.2), 0.1, 1.0)
    gate_w = normal_values(splits[3], (EXPERTS, D, FF), D ** -0.5, 0.09375, ((0, 16), (2, 2)))
    up_w = normal_values(splits[4], (EXPERTS, D, FF), D ** -0.5, 0.09375, ((0, 16), (2, 2)))
    down_w = normal_values(splits[5], (EXPERTS, FF, D), FF ** -0.5, 0.15625, ((0, 16), (1, 2)))
    return dict(tokens=tokens, expert_ids=expert_ids, route_weights=route_weights, gate_w=gate_w, up_w=up_w, down_w=down_w)


def reference(tokens, expert_ids, route_weights, gate_w, up_w, down_w):
    total_rows = tokens.shape[0]
    blocks = total_rows // TOK_DEV
    grouped = expert_ids.reshape(blocks, TOK_DEV * TOP)
    onehot = (grouped[:, :, None] == jnp.arange(EXPERTS, dtype=jnp.int32)[None, None, :]).astype(jnp.int32)
    before = jnp.cumsum(onehot, axis=1) - onehot
    slot = jnp.sum(before * onehot, axis=2)
    block_index = jnp.arange(blocks, dtype=jnp.int32)[:, None]
    position = (block_index * CAP + slot).reshape(-1).astype(jnp.int32)
    flat_ids = expert_ids.reshape(-1)
    flat_weights = route_weights.reshape(-1)
    token_index = (jnp.arange(total_rows * TOP, dtype=jnp.int32) // TOP).astype(jnp.int32)
    quarter = FF // 4
    outside = blocks * CAP

    def step(accum, expert):
        chosen = flat_ids == expert
        target = jnp.where(chosen, position, outside).astype(jnp.int32)
        source = jnp.zeros((outside,), jnp.int32).at[target].set(token_index, mode="drop")
        filled = jnp.zeros((outside,), jnp.bool_).at[target].set(True, mode="drop")
        rows = jnp.where(filled[:, None], tokens[source], jnp.zeros((), tokens.dtype))
        gate = jnp.dot(rows, gate_w[expert], preferred_element_type=jnp.float32)
        up_part = jnp.dot(rows, up_w[expert], preferred_element_type=jnp.float32)
        hidden = (jax.nn.silu(gate) * up_part).astype(jnp.bfloat16)
        summed = jnp.zeros((outside, D), jnp.float32)
        for block in range(4):
            piece = jnp.dot(hidden[:, block * quarter:(block + 1) * quarter],
                            down_w[expert][block * quarter:(block + 1) * quarter],
                            preferred_element_type=jnp.float32).astype(jnp.bfloat16)
            piece = lax.optimization_barrier(piece)
            summed = summed + piece.astype(jnp.float32)
        expert_out = summed.astype(jnp.bfloat16)
        weight_pick = jnp.where(chosen, flat_weights, jnp.zeros((), flat_weights.dtype)).reshape(total_rows, TOP)
        where_rows = jnp.where(chosen, position, 0).astype(jnp.int32).reshape(total_rows, TOP)
        for choice_index in range(TOP):
            fetched = expert_out[where_rows[:, choice_index]].astype(jnp.float32)
            accum = accum + weight_pick[:, choice_index][:, None].astype(jnp.float32) * fetched
        return accum, None

    start = jnp.zeros((total_rows, D), jnp.float32)
    result, unused = lax.scan(step, start, jnp.arange(EXPERTS, dtype=jnp.int32))
    return result.astype(jnp.bfloat16)
```

```python
import jax
import jax.numpy as jnp
from jax import lax
from jax.experimental import pallas as pl
from jax.experimental.pallas import tpu as pltpu
from jax.sharding import PartitionSpec as P

MESH = pl.DeviceIdType.MESH
F32, BF16 = jnp.float32, jnp.bfloat16
BASE = 184
TOP = 64
(UP, UP_LAST, DOWN, TOK_A, TOK_B0, TOK_B1, TOK_BO, TOK_X, OWN0, OWN1, SEND_X, SEND_Y, SUM_X, SUM_Y, SUM_YX,
 CHAIN_C, CHAIN_O, CHAIN_B, END_O, END_C, END_B) = (0,) + tuple(range(2, 22))
WORDS = (
    (
        49850824, 150665288, 358073058, 56111586, 647942769, 368730306, 164272721, 20973284,
        121409692, 237128265, 813427963, 383356677, 433636182, 573555470, 87438293, 673536639,
        633045140, 585823495, 913642263, 688750119, 894598566, 740115069, 788024453, 871100862,
        1102382432,
    ),
    (
        62377914, 219257362, 400185306, 425375675, 50960272, 74892483, 126964453, 356641131,
        6884756, 171187214, 243155517, 109426654, 393475451, 83392022, 96457053, 144278374,
        595363578, 695289367, 739162868, 788090508, 894530854, 926188378, 881974099, 970671378,
        1102381312,
    ),
    (
        74905004, 231649764, 437630412, 412850061, 88539334, 62366869, 114303411, 393815389,
        44330594, 183848984, 205576459, 147005704, 355894925, 70730976, 59282059, 106834736,
        558188588, 658115841, 701988610, 750645402, 857085744, 913662764, 869583909, 982927620,
        1102381686,
    ),
    (
        87432094, 188111134, 395654324, 93692116, 685387143, 381258132, 176664391, 33501106,
        133936778, 199683167, 825954317, 370965011, 421379200, 561028376, 49859235, 660874121,
        620652738, 548242225, 926167873, 651168849, 857018032, 702669963, 750714771, 883763368,
        1102383542,
    ),
)


def place():
    e = lax.axis_index("expert")
    return e, e // 4, (e // 2) % 2, e % 2, lax.axis_index("tensor")


def dev(z, y, c, x):
    return {"expert": (z * 2 + y) * 2 + c, "tensor": x}


def word_at(z, i):
    out = jnp.int32(0)
    for k, column in enumerate(zip(*WORDS)):
        w = jnp.int32(column[3])
        for zz in range(3):
            w = jnp.where(z == zz, jnp.int32(column[zz]), w)
        out = jnp.where(i == k, w, out)
    return out


def layer_kernel(
    tok, wts, gate_hbm, up_hbm, down_hbm, out,
    held, gate_v, up_v, down_v, wall, wcol, hbuf, hsend, got_x, got_y, got_yx, got_c, got_o, got_b, got_end,
    load_s, wsend, wrecv, za_s, zb_s, ya_s, yb_s, x_s, ca_s, cb_s, h_s, dn_s,
    a_r, b_r, x_r, ca_r, cb_r, h_r, dn_r,
    sx_s, sx_r, sy_s, sy_r, yx_s, yx_r, kc_s, kc_r, ko_s, ko_r, kb_s, kb_r, en_s, en_r,
):
    e, z, y, c, x = place()
    n_dev = wall.shape[0]
    rows, width = held.shape[1], held.shape[2]
    units = gate_v.shape[1]
    part = rows // 4
    top = got_x.shape[1]
    half = width // 2
    above, below = dev(jnp.minimum(z + 1, 3), y, c, x), dev(jnp.maximum(z - 1, 0), y, c, x)
    peer_c, peer_x, peer_y = dev(z, y, 1 - c, x), dev(z, y, c, 1 - x), dev(z, 1 - y, c, x)
    keep = pl.ds(pl.multiple_of(x * half, 128), half)
    give = pl.ds(pl.multiple_of((1 - x) * half, 128), half)
    ra, rb = pl.ds(0, top), pl.ds(top, rows - top)
    rows_a = pl.ds(pl.multiple_of(x * (rows - part), 16), part)
    rows_x = pl.ds(pl.multiple_of((1 - x) * (rows - part), 16), part)
    rows_main = pl.ds(pl.multiple_of(x * part, 16), rows - part)

    def rcopy(src, dst, send, recv, target):
        return pltpu.make_async_remote_copy(
            src_ref=src, dst_ref=dst, send_sem=send, recv_sem=recv, device_id=target, device_id_type=MESH
        )

    load_own = pltpu.make_async_copy(tok, held.at[e], load_s.at[0])
    load_w = pltpu.make_async_copy(wts, wall.at[e], load_s.at[1])
    load_gate = pltpu.make_async_copy(gate_hbm.at[0], gate_v, load_s.at[2])
    load_up = pltpu.make_async_copy(up_hbm.at[0], up_v, load_s.at[3])
    mine = pl.ds(pl.multiple_of(c * units, 128), units)
    theirs = pl.ds(pl.multiple_of((1 - c) * units, 128), units)
    load_down = pltpu.make_async_copy(down_hbm.at[0], down_v.at[mine], load_s.at[4])
    load_own.start()
    load_w.start()
    load_gate.start()
    load_up.start()
    load_down.start()

    barrier = pltpu.get_barrier_semaphore()

    def greet(k, carry):
        pl.semaphore_signal(
            barrier, inc=1, device_id={"expert": (e + k) % n_dev, "tensor": x}, device_id_type=MESH
        )
        return carry

    lax.fori_loop(1, n_dev, greet, 0)
    pl.semaphore_signal(barrier, inc=1, device_id=peer_x, device_id_type=MESH)
    pl.semaphore_wait(barrier, n_dev)

    def tok_copy(q, part_rows, send, recv, target):
        ref = held.at[q * 2 + c, part_rows]
        return rcopy(ref, ref, send, recv, target)

    def b_rows(h):
        return pl.ds(part * (1 + h), part)

    def a_up(q):
        return tok_copy(q, rows_a, za_s.at[0, q], a_r.at[q], above)

    def a_down(q):
        return tok_copy(q, rows_a, za_s.at[1, q], a_r.at[q], below)

    def a_y(q):
        return tok_copy(q, rows_a, ya_s.at[0], a_r.at[q], peer_y)

    def b_up(q, h):
        return tok_copy(q, b_rows(h), zb_s.at[0, q // 2, h], b_r.at[q, h], above)

    def b_down(q, h):
        return tok_copy(q, b_rows(h), zb_s.at[1, q // 2, h], b_r.at[q, h], below)

    def b_y(q, h):
        return tok_copy(q, b_rows(h), yb_s.at[q // 2, h], b_r.at[q, h], peer_y)

    def x_copy(q):
        return tok_copy(q, rows_a, x_s.at[q], x_r.at[q], peer_x)

    def x_arrive(q):
        return tok_copy(q, rows_x, x_s.at[q], x_r.at[q], peer_x)

    def core_copy(q, lane):
        ref = held.at[q * 2 + lane, rows_main]
        return rcopy(ref, ref, ca_s.at[q], ca_r.at[q], peer_c)

    def core_x_copy(q, lane):
        ref = held.at[q * 2 + lane, rows_x]
        return rcopy(ref, ref, cb_s.at[q], cb_r.at[q], peer_c)

    def h_copy(q):
        return rcopy(hsend.at[q], hbuf.at[q, :, mine], h_s.at[q], h_r.at[q], peer_c)

    def h_arrive(q):
        return rcopy(hsend.at[q], hbuf.at[q, :, theirs], h_s.at[q], h_r.at[q], peer_c)

    def down_copy(where):
        return rcopy(down_hbm.at[0], down_v.at[where], dn_s.at[0], dn_r.at[0], peer_c)

    def w_copy(k):
        return rcopy(
            wall.at[e], wall.at[e], wsend.at[k], wrecv.at[k], {"expert": (e + k) % n_dev, "tensor": x}
        )

    def w_arrive(k):
        ref = wall.at[(e + n_dev - k) % n_dev]
        return rcopy(ref, ref, wsend.at[k], wrecv.at[k], {"expert": (e + k) % n_dev, "tensor": x})

    def sums(q):
        return q * 2 + 1 - c

    def sx_copy(q):
        return rcopy(held.at[sums(q), ra, give], got_x.at[q], sx_s.at[q], sx_r.at[q], peer_x)

    def sy_copy(t, q):
        return rcopy(held.at[sums(q), rb], got_y.at[t], sy_s.at[t], sy_r.at[t], peer_y)

    def yx_copy(t, q):
        return rcopy(held.at[sums(q), rb, give], got_yx.at[t], yx_s.at[t], yx_r.at[t], peer_x)

    def end_copy(q):
        return rcopy(held.at[sums(q), ra, keep], got_end, en_s.at[0], en_r.at[0], peer_y)

    chains = ((got_c, kc_s, kc_r, ra), (got_o, ko_s, ko_r, ra), (got_b, kb_s, kb_r, rb))

    def chain_up(kind, t, q):
        got, s, r, part_rows = chains[kind]
        return rcopy(held.at[sums(q), part_rows, keep], got.at[t], s.at[t], r.at[t], above)

    def chain_down(kind, t, q):
        got, s, r, part_rows = chains[kind]
        slot = jnp.where(t == z - 1, 4, t)
        return rcopy(held.at[sums(q), part_rows, keep], got.at[slot], s.at[t], r.at[slot], below)

    def chain_arrive(kind, slot, q):
        got, s, r, part_rows = chains[kind]
        return rcopy(held.at[sums(q), part_rows, keep], got.at[slot], s.at[0], r.at[slot], below)

    def add(q, r, cols, other):
        s = sums(q)
        held[s, r, cols] = (held[s, r, cols].astype(F32) + other.astype(F32)).astype(BF16)

    me = z * 2 + y
    load_own.wait()

    @pl.when(z < 3)
    def _():
        a_up(me).start()

    @pl.when(z > 0)
    def _():
        a_down(me).start()

    a_y(me).start()
    core_copy(me, c).start()
    core_x_copy(me, c).start()
    b_y(me, 0).start()
    b_y(me, 1).start()
    load_w.wait()

    def send_w(k, carry):
        w_copy(k).start()
        return carry

    lax.fori_loop(1, n_dev, send_w, 0)
    down_copy(mine).start()

    def got_w(k, carry):
        w_arrive(k).wait_recv()
        return carry

    def forward_b(q, zz, h):
        @pl.when((zz <= z) & (z < 3))
        def _():
            b_up(q, h).start()

        @pl.when((zz >= z) & (z > 0))
        def _():
            b_down(q, h).start()

    def run(step):
        kind = step // 8
        zz = (step // 2) % 4
        r = step % 2
        q = zz * 2 + jnp.where(r == 0, y, 1 - y)

        def on(k):
            return pl.when(kind == k)

        @pl.when(kind < DOWN)
        def _():
            @on(UP)
            def _():
                core_copy(q, 1 - c).wait_recv()
                core_x_copy(q, 1 - c).wait_recv()

            n = pl.multiple_of(kind * 256, 256)
            a = jnp.concatenate([held[q * 2 + c], held[q * 2 + 1 - c]], axis=0)
            w = jnp.concatenate([wcol[q * 2 + c], wcol[q * 2 + 1 - c]], axis=0)
            g = jnp.dot(a, gate_v[:, pl.ds(n, 256)], preferred_element_type=F32)
            u = jnp.dot(a, up_v[:, pl.ds(n, 256)], preferred_element_type=F32)
            h = (g / (1.0 + jnp.exp(-g)) * u * w).astype(BF16)
            hbuf[q, :, pl.ds(pl.multiple_of(c * units + n, 256), 256)] = h[:rows]
            hsend[q, :, pl.ds(n, 256)] = h[rows:]

            @on(UP_LAST)
            def _():
                h_copy(q).start()

        @on(DOWN)
        def _():
            h_arrive(q).wait_recv()
            h = hbuf[q]
            for n in range(0, width, 512):
                p = jnp.dot(h, down_v[:, n:n + 512], preferred_element_type=F32)
                held[sums(q), :, n:n + 512] = p.astype(BF16)

        @pl.when((kind > DOWN) & (kind < SEND_X))
        def _():
            @on(TOK_A)
            def _():
                a_y(q).wait_recv()

                @pl.when((zz <= z) & (z < 3))
                def _():
                    a_up(q).start()

                @pl.when((zz >= z) & (z > 0))
                def _():
                    a_down(q).start()

                x_copy(q).start()

            @pl.when((kind == TOK_B0) | (kind == TOK_B1))
            def _():
                h = kind - TOK_B0
                b_y(q, h).wait_recv()
                forward_b(q, zz, h)
                b_y(q, h).start()

            @on(TOK_BO)
            def _():
                b_y(q, 0).wait_recv()
                b_y(q, 1).wait_recv()

            @pl.when((kind == TOK_B1) | (kind == TOK_BO))
            def _():
                core_copy(q, c).start()

            @on(TOK_X)
            def _():
                x_arrive(q).wait_recv()
                core_x_copy(q, c).start()

            @pl.when(kind >= OWN0)
            def _():
                forward_b(q, zz, kind - OWN0)

        @pl.when((kind >= SEND_X) & (kind < CHAIN_C))
        def _():
            @on(SEND_X)
            def _():
                sx_copy(q).start()

            @on(SEND_Y)
            def _():
                sy_copy(zz, q).start()

            @on(SUM_X)
            def _():
                sx_copy(q).wait_recv()
                add(q, ra, keep, got_x[q])

            @on(SUM_Y)
            def _():
                sy_copy(zz, q).wait_recv()
                add(q, rb, slice(None), got_y[zz])
                yx_copy(zz, q).start()

            @on(SUM_YX)
            def _():
                yx_copy(zz, q).wait_recv()
                add(q, rb, keep, got_yx[zz])

        def chain(i):
            got, _, _, part_rows = chains[i]

            @pl.when(((zz > z) & (z > 0)) | ((zz < z) & (z < 3)))
            def _():
                chain_arrive(i, zz, q).wait_recv()
                add(q, part_rows, keep, got[zz])

            @pl.when(zz > z)
            def _():
                chain_up(i, zz, q).start()

            @pl.when(zz < z)
            def _():
                chain_down(i, zz, q).start()

        def finish(i):
            got, _, _, part_rows = chains[i]

            @pl.when(z > 0)
            def _():
                chain_arrive(i, z, q).wait_recv()
                add(q, part_rows, keep, got[z])

            @pl.when(z < 3)
            def _():
                chain_arrive(i, 4, q).wait_recv()
                add(q, part_rows, keep, got[4])

        @pl.when((kind >= CHAIN_C) & (kind <= END_B))
        def _():
            for i, k in enumerate((CHAIN_C, CHAIN_O, CHAIN_B)):
                @on(k)
                def _():
                    chain(i)

            @on(END_O)
            def _():
                finish(1)
                end_copy(q).start()

            @on(END_C)
            def _():
                finish(0)
                end_copy(q).wait_recv()
                add(q, ra, keep, got_end[...])
                out[ra] = held[sums(q), ra, keep]

            @on(END_B)
            def _():
                finish(2)
                out[rb] = held[sums(q), rb, keep]

    lax.fori_loop(1, n_dev, got_w, 0)

    def weigh(k, carry):
        experts = wall.shape[1]
        col = lax.broadcasted_iota(jnp.int32, (rows, experts), 1) == e
        wcol[k] = jnp.sum(jnp.where(col, wall[k].T, 0.0), axis=1, keepdims=True)
        return carry

    lax.fori_loop(0, n_dev, weigh, 0)
    load_gate.wait()
    load_up.wait()
    load_down.wait()
    down_copy(theirs).wait_recv()

    def steps(i, carry):
        word = word_at(z, i)

        def one(k, rest):
            run(rest % BASE)
            return rest // BASE

        lax.fori_loop(0, 4, one, word)
        return carry

    lax.fori_loop(0, len(WORDS[0]), steps, 0)

    def drain_w(k, carry):
        w_copy(k).wait_send()
        return carry

    lax.fori_loop(1, n_dev, drain_w, 0)
    down_copy(mine).wait_send()
    a_y(me).wait_send()

    def drain(q, carry):
        zz = q // 2
        own_row = q % 2 == y

        @pl.when((zz <= z) & (z < 3))
        def _():
            a_up(q).wait_send()

            @pl.when(own_row)
            def _():
                b_up(q, 0).wait_send()
                b_up(q, 1).wait_send()

        @pl.when((zz >= z) & (z > 0))
        def _():
            a_down(q).wait_send()

            @pl.when(own_row)
            def _():
                b_down(q, 0).wait_send()
                b_down(q, 1).wait_send()

        @pl.when(q != me)
        def _():
            x_copy(q).wait_send()

        core_copy(q, c).wait_send()
        core_x_copy(q, c).wait_send()
        h_copy(q).wait_send()
        sx_copy(q).wait_send()

        @pl.when(own_row)
        def _():
            b_y(q, 0).wait_send()
            b_y(q, 1).wait_send()
            yx_copy(zz, q).wait_send()

        @pl.when(~own_row)
        def _():
            sy_copy(zz, q).wait_send()

        for i in range(3):
            @pl.when((own_row if i != 1 else ~own_row) & (zz > z))
            def _():
                chain_up(i, zz, q).wait_send()

            @pl.when((own_row if i != 1 else ~own_row) & (zz < z))
            def _():
                chain_down(i, zz, q).wait_send()

        return carry

    lax.fori_loop(0, 8, drain, 0)
    end_copy(z * 2 + 1 - y).wait_send()


def dense_weights(expert_ids, route_weights, experts):
    hit = expert_ids[None] == jnp.arange(experts, dtype=jnp.int32)[:, None, None]
    return jnp.sum(jnp.where(hit, route_weights[None], 0.0), axis=2)


def on_box(tokens, expert_ids, route_weights, gate_w, up_w, down_w):
    rows, width = tokens.shape
    n_dev = lax.axis_size("expert")
    units = gate_w.shape[2]
    wts = dense_weights(expert_ids, route_weights, n_dev)
    any_ = pl.BlockSpec(memory_space=pl.ANY)
    vmem = pl.BlockSpec(memory_space=pltpu.VMEM)
    sem = lambda *s: pltpu.SemaphoreType.DMA(s)
    buf = lambda *s: pltpu.VMEM(s, BF16)
    half = width // 2
    top = TOP
    low = rows - top
    return pl.pallas_call(
        layer_kernel,
        out_shape=jax.ShapeDtypeStruct((rows, half), BF16),
        in_specs=[any_] * 5,
        out_specs=vmem,
        scratch_shapes=[
            buf(n_dev, rows, width), buf(width, units), buf(width, units), buf(2 * units, width),
            pltpu.VMEM((n_dev, n_dev, rows), F32), pltpu.VMEM((n_dev, rows, 1), F32),
            buf(8, rows, 2 * units), buf(8, rows, units),
            buf(8, top, half), buf(4, low, width), buf(4, low, half),
            buf(5, top, half), buf(5, top, half), buf(5, low, half), buf(top, half),
            sem(5), sem(n_dev), sem(n_dev), sem(2, 8), sem(2, 4, 2), sem(1), sem(4, 2), sem(8),
            sem(8), sem(8), sem(8), sem(1),
            sem(8), sem(8, 2), sem(8), sem(8), sem(8), sem(8), sem(1),
            sem(8), sem(8), sem(4), sem(4), sem(4), sem(4),
            sem(4), sem(5), sem(4), sem(5), sem(4), sem(5), sem(1), sem(1),
        ],
        compiler_params=pltpu.CompilerParams(
            collective_id=0, has_side_effects=True, vmem_limit_bytes=62 * 2**20
        ),
        name="moe_layer",
    )(tokens, wts, gate_w, up_w, down_w)


def anywhere(tokens, expert_ids, route_weights, gate_w, up_w, down_w):
    rows, width = tokens.shape
    local_experts = gate_w.shape[0]
    experts = local_experts * lax.axis_size("expert")
    first = lax.axis_index("expert") * local_experts
    wts = dense_weights(expert_ids, route_weights, experts)
    every = lax.all_gather(tokens, "expert", axis=0, tiled=True)
    wall = lax.all_gather(wts, "expert", axis=1, tiled=True)
    total = None
    for i in range(local_experts):
        w = lax.dynamic_index_in_dim(wall, first + i, 0, keepdims=False)[:, None]
        g = jnp.dot(every, gate_w[i], preferred_element_type=F32)
        u = jnp.dot(every, up_w[i], preferred_element_type=F32)
        h = (jax.nn.silu(g) * u * w).astype(BF16)
        p = jnp.dot(h, down_w[i], preferred_element_type=F32)
        total = p if total is None else total + p
    mixed = lax.psum_scatter(total.astype(BF16), "expert", scatter_dimension=0, tiled=True)
    return lax.psum_scatter(mixed, "tensor", scatter_dimension=1, tiled=True)


def solution(mesh):
    shape = dict(mesh.shape)
    box = shape == {"groups": 1, "expert": 16, "tensor": 2}
    in_specs = (
        P(("groups", "expert"), None),
        P(("groups", "expert"), None),
        P(("groups", "expert"), None),
        P("expert", None, "tensor"),
        P("expert", None, "tensor"),
        P("expert", "tensor", None),
    )
    out_specs = P(("groups", "expert"), "tensor")
    return jax.shard_map(
        on_box if box else anywhere, mesh=mesh, in_specs=in_specs, out_specs=out_specs, check_vma=False
    )
```

```python
import jax
import jax.numpy as jnp
from jax import lax
from jax.experimental import pallas as pl
from jax.experimental.pallas import tpu as pltpu
from jax.sharding import PartitionSpec as P

MESH = pl.DeviceIdType.MESH
F32, BF16 = jnp.float32, jnp.bfloat16
BASE = 200
TOP = 48
FAR = 2
(UP, UP_LAST, DOWN, TOK_A, TOK_B0, TOK_B1, TOK_BO, TOK_X, OWN0, OWN1, SEND_X, SEND_Y, SUM_X, SUM_Y, SUM_YX,
 CHAIN_C, CHAIN_O, CHAIN_B, END_O, END_C, END_B, GOT_W, GOT_DOWN) = (0,) + tuple(range(2, 24))
WORDS = (
    (
        7056072, 273323208, 521684984, 531530057, 17401801, 136722104, 537047259, 712128825,
        296773611, 36205452, 161538212, 369132269, 312842605, 565570907, 115721229, 506844501,
        60366092, 1128923094, 1057258108, 851822103, 1044463334, 948979943, 782025348, 1229864514,
        1348832112,
    ),
    (
        23056474, 281283610, 321076836, 418372844, 305333448, 88133600, 96167419, 488805465,
        130801646, 722171428, 704053824, 168521009, 504699839, 201161306, 178842889, 809201504,
        844564615, 828898631, 933661895, 780978311, 949741494, 741506910, 1029071148, 966021712,
        1366508932,
    ),
    (
        39056876, 297524012, 337156834, 402454046, 313293854, 104213206, 80087021, 472725864,
        178842840, 737932626, 752293430, 152440615, 456940233, 249080108, 130601695, 792960310,
        892643409, 780978225, 917581489, 828898705, 901501888, 725745704, 1076831546, 1013781318,
        1382590130,
    ),
    (
        55057278, 289564414, 569766184, 547770463, 33483007, 184802510, 553126861, 760208431,
        280853213, 20445850, 145298610, 321051867, 264762203, 517649709, 67640027, 458603299,
        12284890, 1112681888, 1041018506, 867580897, 1060222928, 900900337, 829784146, 1277944916,
        1397073318,
    ),
)


def place():
    e = lax.axis_index("expert")
    return e, e // 4, (e // 2) % 2, e % 2, lax.axis_index("tensor")


def dev(z, y, c, x):
    return {"expert": (z * 2 + y) * 2 + c, "tensor": x}


def word_at(z, i):
    out = jnp.int32(0)
    for k, column in enumerate(zip(*WORDS)):
        w = jnp.int32(column[3])
        for zz in range(3):
            w = jnp.where(z == zz, jnp.int32(column[zz]), w)
        out = jnp.where(i == k, w, out)
    return out


def layer_kernel(
    tok, ids_hbm, route_hbm, gate_hbm, up_hbm, down_hbm, out,
    held, gate_v, up_v, down_v, wall, wcol, wblk, ids_v, route_v, hbuf, hsend, got_x, got_y, got_yx, got_c, got_o, got_b, got_end,
    load_s, wsend, wrecv, za_s, zb_s, ya_s, yb_s, x_s, ca_s, cb_s, h_s, dn_s,
    a_r, b_r, x_r, ca_r, cb_r, h_r, dn_r,
    sx_s, sx_r, sy_s, sy_r, yx_s, yx_r, kc_s, kc_r, ko_s, ko_r, kb_s, kb_r, en_s, en_r,
):
    e, z, y, c, x = place()
    n_dev = wall.shape[0]
    rows, width = held.shape[1], held.shape[2]
    units = gate_v.shape[1]
    part = rows // 4
    top = got_x.shape[1]
    half = width // 2
    above, below = dev(jnp.minimum(z + 1, 3), y, c, x), dev(jnp.maximum(z - 1, 0), y, c, x)
    peer_c, peer_x, peer_y = dev(z, y, 1 - c, x), dev(z, y, c, 1 - x), dev(z, 1 - y, c, x)
    keep = pl.ds(pl.multiple_of(x * half, 128), half)
    give = pl.ds(pl.multiple_of((1 - x) * half, 128), half)
    ra, rb = pl.ds(0, top), pl.ds(top, rows - top)
    rows_a = pl.ds(pl.multiple_of(x * (rows - part), 16), part)
    rows_x = pl.ds(pl.multiple_of((1 - x) * (rows - part), 16), part)
    rows_main = pl.ds(pl.multiple_of(x * part, 16), rows - part)

    def rcopy(src, dst, send, recv, target):
        return pltpu.make_async_remote_copy(
            src_ref=src, dst_ref=dst, send_sem=send, recv_sem=recv, device_id=target, device_id_type=MESH
        )

    load_own = pltpu.make_async_copy(tok, held.at[e], load_s.at[0])
    load_ids = pltpu.make_async_copy(ids_hbm, ids_v, load_s.at[1])
    load_route = pltpu.make_async_copy(route_hbm, route_v, load_s.at[5])
    load_gate = pltpu.make_async_copy(gate_hbm.at[0], gate_v, load_s.at[2])
    load_up = pltpu.make_async_copy(up_hbm.at[0], up_v, load_s.at[3])
    mine = pl.ds(pl.multiple_of(c * units, 128), units)
    theirs = pl.ds(pl.multiple_of((1 - c) * units, 128), units)
    load_down = pltpu.make_async_copy(down_hbm.at[0], down_v.at[mine], load_s.at[4])
    load_own.start()
    load_ids.start()
    load_route.start()
    load_gate.start()
    load_up.start()
    load_down.start()

    barrier = pltpu.get_barrier_semaphore()

    def greet(k, carry):
        pl.semaphore_signal(
            barrier, inc=1, device_id={"expert": (e + k) % n_dev, "tensor": x}, device_id_type=MESH
        )
        return carry

    lax.fori_loop(1, n_dev, greet, 0)
    pl.semaphore_signal(barrier, inc=1, device_id=peer_x, device_id_type=MESH)
    load_ids.wait()
    load_route.wait()
    experts = wall.shape[1]
    lane = lax.broadcasted_iota(jnp.int32, (rows, experts), 1)
    dense = jnp.zeros((rows, experts), F32)
    for k in range(ids_v.shape[1]):
        dense = dense + jnp.where(ids_v[:, k:k + 1] == lane, route_v[:, k:k + 1], 0.0)
    wall[e] = dense.T
    pl.semaphore_wait(barrier, n_dev)

    def tok_copy(q, part_rows, send, recv, target):
        ref = held.at[q * 2 + c, part_rows]
        return rcopy(ref, ref, send, recv, target)

    def b_rows(h):
        return pl.ds(part * (1 + h), part)

    def a_up(q):
        return tok_copy(q, rows_a, za_s.at[0, q], a_r.at[q], above)

    def a_down(q):
        return tok_copy(q, rows_a, za_s.at[1, q], a_r.at[q], below)

    def a_y(q):
        return tok_copy(q, rows_a, ya_s.at[q // 2], a_r.at[q], peer_y)

    def a_goes_up(zz, r):
        return (zz <= z) & (z < 3) & ((r == 0) | (z < 2) | (zz > 3 - FAR))

    def a_goes_down(zz, r):
        return (zz >= z) & (z > 0) & ((r == 0) | (z > 1) | (zz < FAR))

    def a_crosses(zz):
        return ((z == 0) & (zz >= FAR)) | ((z == 3) & (zz <= 3 - FAR)) | (zz == z)

    def b_up(q, h):
        return tok_copy(q, b_rows(h), zb_s.at[0, q // 2, h], b_r.at[q, h], above)

    def b_down(q, h):
        return tok_copy(q, b_rows(h), zb_s.at[1, q // 2, h], b_r.at[q, h], below)

    def b_y(q, h):
        return tok_copy(q, b_rows(h), yb_s.at[q // 2, h], b_r.at[q, h], peer_y)

    def x_copy(q):
        return tok_copy(q, rows_a, x_s.at[q], x_r.at[q], peer_x)

    def x_arrive(q):
        return tok_copy(q, rows_x, x_s.at[q], x_r.at[q], peer_x)

    def core_copy(q, lane):
        ref = held.at[q * 2 + lane, rows_main]
        return rcopy(ref, ref, ca_s.at[q], ca_r.at[q], peer_c)

    def core_x_copy(q, lane):
        ref = held.at[q * 2 + lane, rows_x]
        return rcopy(ref, ref, cb_s.at[q], cb_r.at[q], peer_c)

    def h_copy(q):
        return rcopy(hsend.at[q], hbuf.at[q, :, mine], h_s.at[q], h_r.at[q], peer_c)

    def h_arrive(q):
        return rcopy(hsend.at[q], hbuf.at[q, :, theirs], h_s.at[q], h_r.at[q], peer_c)

    def down_copy(where):
        return rcopy(down_hbm.at[0], down_v.at[where], dn_s.at[0], dn_r.at[0], peer_c)

    def w_copy(k):
        return rcopy(
            wall.at[e], wall.at[e], wsend.at[k], wrecv.at[k], {"expert": (e + k) % n_dev, "tensor": x}
        )

    def w_arrive(k):
        ref = wall.at[(e + n_dev - k) % n_dev]
        return rcopy(ref, ref, wsend.at[k], wrecv.at[k], {"expert": (e + k) % n_dev, "tensor": x})

    def sums(q):
        return q * 2 + 1 - c

    def sx_copy(q):
        return rcopy(held.at[sums(q), ra, give], got_x.at[q], sx_s.at[q], sx_r.at[q], peer_x)

    def sy_copy(t, q):
        return rcopy(held.at[sums(q), rb], got_y.at[t], sy_s.at[t], sy_r.at[t], peer_y)

    def yx_copy(t, q):
        return rcopy(held.at[sums(q), rb, give], got_yx.at[t], yx_s.at[t], yx_r.at[t], peer_x)

    def end_copy(q):
        return rcopy(held.at[sums(q), ra, keep], got_end, en_s.at[0], en_r.at[0], peer_y)

    chains = ((got_c, kc_s, kc_r, ra), (got_o, ko_s, ko_r, ra), (got_b, kb_s, kb_r, rb))

    def chain_up(kind, t, q):
        got, s, r, part_rows = chains[kind]
        return rcopy(held.at[sums(q), part_rows, keep], got.at[t], s.at[t], r.at[t], above)

    def chain_down(kind, t, q):
        got, s, r, part_rows = chains[kind]
        slot = jnp.where(t == z - 1, 4, t)
        return rcopy(held.at[sums(q), part_rows, keep], got.at[slot], s.at[t], r.at[slot], below)

    def chain_arrive(kind, slot, q):
        got, s, r, part_rows = chains[kind]
        return rcopy(held.at[sums(q), part_rows, keep], got.at[slot], s.at[0], r.at[slot], below)

    def add(q, r, cols, other):
        s = sums(q)
        held[s, r, cols] = (held[s, r, cols].astype(F32) + other.astype(F32)).astype(BF16)

    me = z * 2 + y
    load_own.wait()

    @pl.when(z < 3)
    def _():
        a_up(me).start()

    @pl.when(z > 0)
    def _():
        a_down(me).start()

    a_y(me).start()
    core_copy(me, c).start()
    core_x_copy(me, c).start()
    b_y(me, 0).start()
    b_y(me, 1).start()
    def send_w(k, carry):
        w_copy(k).start()
        return carry

    lax.fori_loop(1, n_dev, send_w, 0)
    down_copy(mine).start()

    def got_w(k, carry):
        w_arrive(k).wait_recv()
        return carry

    def forward_b(q, zz, h):
        @pl.when((zz <= z) & (z < 3))
        def _():
            b_up(q, h).start()

        @pl.when((zz >= z) & (z > 0))
        def _():
            b_down(q, h).start()

    def run(step):
        kind = step // 8
        zz = (step // 2) % 4
        r = step % 2
        q = zz * 2 + jnp.where(r == 0, y, 1 - y)

        def on(k):
            return pl.when(kind == k)

        @pl.when(kind < DOWN)
        def _():
            @on(UP)
            def _():
                core_copy(q, 1 - c).wait_recv()
                core_x_copy(q, 1 - c).wait_recv()
                chunk = lax.broadcasted_iota(jnp.int32, (rows, n_dev), 1)
                for i, s in enumerate((q * 2 + c, q * 2 + 1 - c)):
                    w = jnp.where(chunk == s, wcol[...], 0.0)
                    wblk[q, rows * i:rows * (i + 1)] = jnp.sum(w, axis=1, keepdims=True)

            n = pl.multiple_of(kind * 256, 256)
            a = jnp.concatenate([held[q * 2 + c], held[q * 2 + 1 - c]], axis=0)
            g = jnp.dot(a, gate_v[:, pl.ds(n, 256)], preferred_element_type=F32)
            u = jnp.dot(a, up_v[:, pl.ds(n, 256)], preferred_element_type=F32)
            h = (g / (1.0 + jnp.exp(-g)) * u * wblk[q]).astype(BF16)
            hbuf[q, :, pl.ds(pl.multiple_of(c * units + n, 256), 256)] = h[:rows]
            hsend[q, :, pl.ds(n, 256)] = h[rows:]

            @on(UP_LAST)
            def _():
                h_copy(q).start()

        @on(DOWN)
        def _():
            h_arrive(q).wait_recv()
            h = hbuf[q]
            for n in range(0, width, 512):
                p = jnp.dot(h, down_v[:, n:n + 512], preferred_element_type=F32)
                held[sums(q), :, n:n + 512] = p.astype(BF16)

        @pl.when((kind > DOWN) & (kind < SEND_X))
        def _():
            @on(TOK_A)
            def _():
                a_y(q).wait_recv()

                @pl.when(a_goes_up(zz, r))
                def _():
                    a_up(q).start()

                @pl.when(a_goes_down(zz, r))
                def _():
                    a_down(q).start()

                @pl.when((r == 0) & a_crosses(zz))
                def _():
                    a_y(q).start()

                x_copy(q).start()

            @pl.when((kind == TOK_B0) | (kind == TOK_B1))
            def _():
                h = kind - TOK_B0
                b_y(q, h).wait_recv()
                forward_b(q, zz, h)
                b_y(q, h).start()

            @on(TOK_BO)
            def _():
                b_y(q, 0).wait_recv()
                b_y(q, 1).wait_recv()

            @pl.when((kind == TOK_B1) | (kind == TOK_BO))
            def _():
                core_copy(q, c).start()

            @on(TOK_X)
            def _():
                x_arrive(q).wait_recv()
                core_x_copy(q, c).start()

            @pl.when(kind >= OWN0)
            def _():
                forward_b(q, zz, kind - OWN0)

        @pl.when((kind >= SEND_X) & (kind < CHAIN_C))
        def _():
            @on(SEND_X)
            def _():
                sx_copy(q).start()

            @on(SEND_Y)
            def _():
                sy_copy(zz, q).start()

            @on(SUM_X)
            def _():
                sx_copy(q).wait_recv()
                add(q, ra, keep, got_x[q])

            @on(SUM_Y)
            def _():
                sy_copy(zz, q).wait_recv()
                add(q, rb, slice(None), got_y[zz])
                yx_copy(zz, q).start()

            @on(SUM_YX)
            def _():
                yx_copy(zz, q).wait_recv()
                add(q, rb, keep, got_yx[zz])

        def chain(i):
            got, _, _, part_rows = chains[i]

            @pl.when(((zz > z) & (z > 0)) | ((zz < z) & (z < 3)))
            def _():
                chain_arrive(i, zz, q).wait_recv()
                add(q, part_rows, keep, got[zz])

            @pl.when(zz > z)
            def _():
                chain_up(i, zz, q).start()

            @pl.when(zz < z)
            def _():
                chain_down(i, zz, q).start()

        def finish(i):
            got, _, _, part_rows = chains[i]

            @pl.when(z > 0)
            def _():
                chain_arrive(i, z, q).wait_recv()
                add(q, part_rows, keep, got[z])

            @pl.when(z < 3)
            def _():
                chain_arrive(i, 4, q).wait_recv()
                add(q, part_rows, keep, got[4])

        @pl.when(kind >= CHAIN_C)
        def _():
            @on(GOT_W)
            def _():
                lax.fori_loop(1, n_dev, got_w, 0)
                expert = lax.broadcasted_iota(jnp.int32, (n_dev, experts, rows), 1)
                wcol[...] = jnp.sum(jnp.where(expert == e, wall[...], 0.0), axis=1).T
                load_gate.wait()
                load_up.wait()

            @on(GOT_DOWN)
            def _():
                load_down.wait()
                down_copy(theirs).wait_recv()

            for i, k in enumerate((CHAIN_C, CHAIN_O, CHAIN_B)):
                @on(k)
                def _():
                    chain(i)

            @on(END_O)
            def _():
                finish(1)
                end_copy(q).start()

            @on(END_C)
            def _():
                finish(0)
                end_copy(q).wait_recv()
                add(q, ra, keep, got_end[...])
                out[ra] = held[sums(q), ra, keep]

            @on(END_B)
            def _():
                finish(2)
                out[rb] = held[sums(q), rb, keep]

    def steps(i, carry):
        word = word_at(z, i)

        def one(k, rest):
            run(rest % BASE)
            return rest // BASE

        lax.fori_loop(0, 4, one, word)
        return carry

    lax.fori_loop(0, len(WORDS[0]), steps, 0)

    def drain_w(k, carry):
        w_copy(k).wait_send()
        return carry

    lax.fori_loop(1, n_dev, drain_w, 0)
    down_copy(mine).wait_send()

    def drain(q, carry):
        zz = q // 2
        own_row = q % 2 == y

        r = jnp.where(own_row, 0, 1)

        @pl.when(a_goes_up(zz, r))
        def _():
            a_up(q).wait_send()

        @pl.when(a_goes_down(zz, r))
        def _():
            a_down(q).wait_send()

        @pl.when(own_row & a_crosses(zz))
        def _():
            a_y(q).wait_send()

        @pl.when(own_row & (zz <= z) & (z < 3))
        def _():
            b_up(q, 0).wait_send()
            b_up(q, 1).wait_send()

        @pl.when(own_row & (zz >= z) & (z > 0))
        def _():
            b_down(q, 0).wait_send()
            b_down(q, 1).wait_send()

        @pl.when(q != me)
        def _():
            x_copy(q).wait_send()

        core_copy(q, c).wait_send()
        core_x_copy(q, c).wait_send()
        h_copy(q).wait_send()
        sx_copy(q).wait_send()

        @pl.when(own_row)
        def _():
            b_y(q, 0).wait_send()
            b_y(q, 1).wait_send()
            yx_copy(zz, q).wait_send()

        @pl.when(~own_row)
        def _():
            sy_copy(zz, q).wait_send()

        for i in range(3):
            @pl.when((own_row if i != 1 else ~own_row) & (zz > z))
            def _():
                chain_up(i, zz, q).wait_send()

            @pl.when((own_row if i != 1 else ~own_row) & (zz < z))
            def _():
                chain_down(i, zz, q).wait_send()

        return carry

    lax.fori_loop(0, 8, drain, 0)
    end_copy(z * 2 + 1 - y).wait_send()


def dense_weights(expert_ids, route_weights, experts):
    hit = expert_ids[None] == jnp.arange(experts, dtype=jnp.int32)[:, None, None]
    return jnp.sum(jnp.where(hit, route_weights[None], 0.0), axis=2)


def on_box(tokens, expert_ids, route_weights, gate_w, up_w, down_w):
    rows, width = tokens.shape
    n_dev = lax.axis_size("expert")
    units = gate_w.shape[2]
    any_ = pl.BlockSpec(memory_space=pl.ANY)
    vmem = pl.BlockSpec(memory_space=pltpu.VMEM)
    sem = lambda *s: pltpu.SemaphoreType.DMA(s)
    buf = lambda *s: pltpu.VMEM(s, BF16)
    half = width // 2
    top = TOP
    low = rows - top
    return pl.pallas_call(
        layer_kernel,
        out_shape=jax.ShapeDtypeStruct((rows, half), BF16),
        in_specs=[any_] * 6,
        out_specs=vmem,
        scratch_shapes=[
            buf(n_dev, rows, width), buf(width, units), buf(width, units), buf(2 * units, width),
            pltpu.VMEM((n_dev, n_dev, rows), F32), pltpu.VMEM((rows, n_dev), F32),
            pltpu.VMEM((8, 2 * rows, 1), F32), pltpu.VMEM(expert_ids.shape, jnp.int32),
            pltpu.VMEM(route_weights.shape, F32),
            buf(8, rows, 2 * units), buf(8, rows, units),
            buf(8, top, half), buf(4, low, width), buf(4, low, half),
            buf(5, top, half), buf(5, top, half), buf(5, low, half), buf(top, half),
            sem(6), sem(n_dev), sem(n_dev), sem(2, 8), sem(2, 4, 2), sem(4), sem(4, 2), sem(8),
            sem(8), sem(8), sem(8), sem(1),
            sem(8), sem(8, 2), sem(8), sem(8), sem(8), sem(8), sem(1),
            sem(8), sem(8), sem(4), sem(4), sem(4), sem(4),
            sem(4), sem(5), sem(4), sem(5), sem(4), sem(5), sem(1), sem(1),
        ],
        compiler_params=pltpu.CompilerParams(
            collective_id=0, has_side_effects=True, vmem_limit_bytes=62 * 2**20
        ),
        name="moe_layer",
    )(tokens, expert_ids, route_weights, gate_w, up_w, down_w)


def anywhere(tokens, expert_ids, route_weights, gate_w, up_w, down_w):
    rows, width = tokens.shape
    local_experts = gate_w.shape[0]
    experts = local_experts * lax.axis_size("expert")
    first = lax.axis_index("expert") * local_experts
    wts = dense_weights(expert_ids, route_weights, experts)
    every = lax.all_gather(tokens, "expert", axis=0, tiled=True)
    wall = lax.all_gather(wts, "expert", axis=1, tiled=True)
    total = None
    for i in range(local_experts):
        w = lax.dynamic_index_in_dim(wall, first + i, 0, keepdims=False)[:, None]
        g = jnp.dot(every, gate_w[i], preferred_element_type=F32)
        u = jnp.dot(every, up_w[i], preferred_element_type=F32)
        h = (jax.nn.silu(g) * u * w).astype(BF16)
        p = jnp.dot(h, down_w[i], preferred_element_type=F32)
        total = p if total is None else total + p
    mixed = lax.psum_scatter(total.astype(BF16), "expert", scatter_dimension=0, tiled=True)
    return lax.psum_scatter(mixed, "tensor", scatter_dimension=1, tiled=True)


def solution(mesh):
    shape = dict(mesh.shape)
    box = shape == {"groups": 1, "expert": 16, "tensor": 2}
    in_specs = (
        P(("groups", "expert"), None),
        P(("groups", "expert"), None),
        P(("groups", "expert"), None),
        P("expert", None, "tensor"),
        P("expert", None, "tensor"),
        P("expert", "tensor", None),
    )
    out_specs = P(("groups", "expert"), "tensor")
    return jax.shard_map(
        on_box if box else anywhere, mesh=mesh, in_specs=in_specs, out_specs=out_specs, check_vma=False
    )
```

```python
import jax
import jax.numpy as jnp
from jax import lax
from jax.experimental import pallas as pl
from jax.experimental.pallas import tpu as pltpu
from jax.sharding import PartitionSpec as P

MESH = pl.DeviceIdType.MESH
F32, BF16 = jnp.float32, jnp.bfloat16
BASE = 208
TOP = 64
FAR = 2
(UP, UP_LAST, DOWN, TOK_A, TOK_B0, TOK_B1, TOK_BO, TOK_X, OWN0, OWN1, SEND_X, SEND_Y, SUM_X, SUM_Y, SUM_YX,
 CHAIN_C, CHAIN_O, CHAIN_B, END_O, END_C, END_B, GOT_W, GOT_DOWN, DRAIN) = (0,) + tuple(range(2, 25))
WORDS = (
    (
        7631176, 298438408, 381766712, 586498706, 936624209, 873985251, 343573657, 490493603,
        353135232, 162413542, 234578708, 644119098, 270487423, 846895927, 182557962, 553065167,
        993866435, 189540758, 177189179, 247015213, 1067605027, 1049996779, 1255509342, 1124195641,
        1319152788, 1808476968,
    ),
    (
        90112330, 289486930, 363855832, 434514540, 343400341, 173750515, 820069166, 144349402,
        218971014, 588485128, 468680785, 873999846, 198583097, 108173211, 553022110, 63223492,
        122268863, 859359301, 841274617, 994745052, 986703439, 1048573071, 1274066900, 1124203102,
        1464256923, 1808476970,
    ),
    (
        108196684, 343566516, 381940600, 488594126, 289666867, 192008341, 838154760, 198602876,
        272879200, 642563886, 450943799, 928253312, 144328799, 90087613, 534765944, 9142242,
        104356313, 805104995, 823189855, 941010746, 968444777, 1030489961, 1256329906, 1106204024,
        1482169469, 1808476972,
    ),
    (
        61625902, 352519662, 400025368, 640406900, 990878519, 928237893, 289493247, 436758469,
        299227878, 180498304, 252315698, 590383964, 216407001, 792641617, 164647084, 534806505,
        939786021, 171455984, 194926173, 264926091, 1013524613, 1031912013, 1273592440, 1106198239,
        1337238386, 1808476974,
    ),
)


def place():
    e = lax.axis_index("expert")
    return e, e // 4, (e // 2) % 2, e % 2, lax.axis_index("tensor")


def dev(z, y, c, x):
    return {"expert": (z * 2 + y) * 2 + c, "tensor": x}


def word_at(z, i):
    out = jnp.int32(0)
    for k, column in enumerate(zip(*WORDS)):
        w = jnp.int32(column[3])
        for zz in range(3):
            w = jnp.where(z == zz, jnp.int32(column[zz]), w)
        out = jnp.where(i == k, w, out)
    return out


def layer_kernel(
    tok, ids_hbm, route_hbm, gate_hbm, up_hbm, down_hbm, out,
    held, gate_v, up_v, down_v, wall, wcol, wblk, ids_v, route_v, hbuf, hsend, got_x, got_y, got_yx, got_c, got_o, got_b, got_end,
    load_s, wsend, wrecv, za_s, zb_s, ya_s, yb_s, x_s, ca_s, cb_s, h_s, dn_s,
    a_r, b_r, x_r, ca_r, cb_r, h_r, dn_r,
    sx_s, sx_r, sy_s, sy_r, yx_s, yx_r, kc_s, kc_r, ko_s, ko_r, kb_s, kb_r, en_s, en_r,
):
    e, z, y, c, x = place()
    n_dev = wall.shape[0]
    rows, width = held.shape[1], held.shape[2]
    units = gate_v.shape[1]
    part = rows // 4
    top = got_x.shape[1]
    half = width // 2
    above, below = dev(jnp.minimum(z + 1, 3), y, c, x), dev(jnp.maximum(z - 1, 0), y, c, x)
    peer_c, peer_x, peer_y = dev(z, y, 1 - c, x), dev(z, y, c, 1 - x), dev(z, 1 - y, c, x)
    keep = pl.ds(pl.multiple_of(x * half, 128), half)
    give = pl.ds(pl.multiple_of((1 - x) * half, 128), half)
    ra, rb = pl.ds(0, top), pl.ds(top, rows - top)
    rows_a = pl.ds(pl.multiple_of(x * (rows - part), 16), part)
    rows_x = pl.ds(pl.multiple_of((1 - x) * (rows - part), 16), part)
    rows_main = pl.ds(pl.multiple_of(x * part, 16), rows - part)

    def rcopy(src, dst, send, recv, target):
        return pltpu.make_async_remote_copy(
            src_ref=src, dst_ref=dst, send_sem=send, recv_sem=recv, device_id=target, device_id_type=MESH
        )

    load_own = pltpu.make_async_copy(tok, held.at[e], load_s.at[0])
    load_ids = pltpu.make_async_copy(ids_hbm, ids_v, load_s.at[1])
    load_route = pltpu.make_async_copy(route_hbm, route_v, load_s.at[5])
    load_gate = pltpu.make_async_copy(gate_hbm.at[0], gate_v, load_s.at[2])
    load_up = pltpu.make_async_copy(up_hbm.at[0], up_v, load_s.at[3])
    mine = pl.ds(pl.multiple_of(c * units, 128), units)
    theirs = pl.ds(pl.multiple_of((1 - c) * units, 128), units)
    load_down = pltpu.make_async_copy(down_hbm.at[0], down_v.at[mine], load_s.at[4])
    load_own.start()
    load_ids.start()
    load_route.start()
    load_gate.start()
    load_up.start()
    load_down.start()

    barrier = pltpu.get_barrier_semaphore()

    def greet(k, carry):
        pl.semaphore_signal(
            barrier, inc=1, device_id={"expert": (e + k) % n_dev, "tensor": x}, device_id_type=MESH
        )
        return carry

    lax.fori_loop(1, n_dev, greet, 0)
    pl.semaphore_signal(barrier, inc=1, device_id=peer_x, device_id_type=MESH)
    load_ids.wait()
    load_route.wait()
    experts = wall.shape[1]
    expert = lax.broadcasted_iota(jnp.int32, (experts, rows), 0)
    dense = jnp.zeros((experts, rows), F32)
    for k in range(ids_v.shape[0]):
        dense = dense + jnp.where(ids_v[k:k + 1] == expert, route_v[k:k + 1], 0.0)
    wall[e] = dense
    pl.semaphore_wait(barrier, n_dev)

    def tok_copy(q, part_rows, send, recv, target):
        ref = held.at[q * 2 + c, part_rows]
        return rcopy(ref, ref, send, recv, target)

    def b_rows(h):
        return pl.ds(part * (1 + h), part)

    def a_up(q):
        return tok_copy(q, rows_a, za_s.at[0, q], a_r.at[q], above)

    def a_down(q):
        return tok_copy(q, rows_a, za_s.at[1, q], a_r.at[q], below)

    def a_y(q):
        return tok_copy(q, rows_a, ya_s.at[q // 2], a_r.at[q], peer_y)

    def a_goes_up(zz, r):
        return (zz <= z) & (z < 3) & ((r == 0) | (z < 2) | (zz > 3 - FAR))

    def a_goes_down(zz, r):
        return (zz >= z) & (z > 0) & ((r == 0) | (z > 1) | (zz < FAR))

    def a_crosses(zz):
        return ((z == 0) & (zz >= FAR)) | ((z == 3) & (zz <= 3 - FAR)) | (zz == z)

    def b_up(q, h):
        return tok_copy(q, b_rows(h), zb_s.at[0, q // 2, h], b_r.at[q, h], above)

    def b_down(q, h):
        return tok_copy(q, b_rows(h), zb_s.at[1, q // 2, h], b_r.at[q, h], below)

    def b_y(q, h):
        return tok_copy(q, b_rows(h), yb_s.at[q // 2, h], b_r.at[q, h], peer_y)

    def x_copy(q):
        return tok_copy(q, rows_a, x_s.at[q], x_r.at[q], peer_x)

    def x_arrive(q):
        return tok_copy(q, rows_x, x_s.at[q], x_r.at[q], peer_x)

    def core_copy(q, lane):
        ref = held.at[q * 2 + lane, rows_main]
        return rcopy(ref, ref, ca_s.at[q], ca_r.at[q], peer_c)

    def core_x_copy(q, lane):
        ref = held.at[q * 2 + lane, rows_x]
        return rcopy(ref, ref, cb_s.at[q], cb_r.at[q], peer_c)

    def h_copy(q):
        return rcopy(hsend.at[q], hbuf.at[q, :, mine], h_s.at[q], h_r.at[q], peer_c)

    def h_arrive(q):
        return rcopy(hsend.at[q], hbuf.at[q, :, theirs], h_s.at[q], h_r.at[q], peer_c)

    def down_copy(where):
        return rcopy(down_hbm.at[0], down_v.at[where], dn_s.at[0], dn_r.at[0], peer_c)

    def w_copy(k):
        return rcopy(
            wall.at[e], wall.at[e], wsend.at[k], wrecv.at[k], {"expert": (e + k) % n_dev, "tensor": x}
        )

    def w_arrive(k):
        ref = wall.at[(e + n_dev - k) % n_dev]
        return rcopy(ref, ref, wsend.at[k], wrecv.at[k], {"expert": (e + k) % n_dev, "tensor": x})

    def sums(q):
        return q * 2 + 1 - c

    def sx_copy(q):
        return rcopy(held.at[sums(q), ra, give], got_x.at[q], sx_s.at[q], sx_r.at[q], peer_x)

    def sy_copy(t, q):
        return rcopy(held.at[sums(q), rb], got_y.at[t], sy_s.at[t], sy_r.at[t], peer_y)

    def yx_copy(t, q):
        return rcopy(held.at[sums(q), rb, give], got_yx.at[t], yx_s.at[t], yx_r.at[t], peer_x)

    def end_copy(q):
        return rcopy(held.at[sums(q), ra, keep], got_end, en_s.at[0], en_r.at[0], peer_y)

    chains = ((got_c, kc_s, kc_r, ra), (got_o, ko_s, ko_r, ra), (got_b, kb_s, kb_r, rb))

    def chain_up(kind, t, q):
        got, s, r, part_rows = chains[kind]
        return rcopy(held.at[sums(q), part_rows, keep], got.at[t], s.at[t], r.at[t], above)

    def chain_down(kind, t, q):
        got, s, r, part_rows = chains[kind]
        slot = jnp.where(t == z - 1, 4, t)
        return rcopy(held.at[sums(q), part_rows, keep], got.at[slot], s.at[t], r.at[slot], below)

    def chain_arrive(kind, slot, q):
        got, s, r, part_rows = chains[kind]
        return rcopy(held.at[sums(q), part_rows, keep], got.at[slot], s.at[0], r.at[slot], below)

    def add(q, r, cols, other):
        s = sums(q)
        held[s, r, cols] = (held[s, r, cols].astype(F32) + other.astype(F32)).astype(BF16)

    me = z * 2 + y
    load_own.wait()

    @pl.when(z < 3)
    def _():
        a_up(me).start()

    @pl.when(z > 0)
    def _():
        a_down(me).start()

    a_y(me).start()
    core_copy(me, c).start()
    core_x_copy(me, c).start()
    b_y(me, 0).start()
    b_y(me, 1).start()
    def send_w(k, carry):
        w_copy(k).start()
        return carry

    lax.fori_loop(1, n_dev, send_w, 0)
    down_copy(mine).start()

    def got_w(k, carry):
        w_arrive(k).wait_recv()
        return carry

    def forward_b(q, zz, h):
        @pl.when((zz <= z) & (z < 3))
        def _():
            b_up(q, h).start()

        @pl.when((zz >= z) & (z > 0))
        def _():
            b_down(q, h).start()

    def drain_w(k, carry):
        w_copy(k).wait_send()
        return carry

    def drain_tokens(q, carry):
        zz = q // 2
        own_row = q % 2 == y

        r = jnp.where(own_row, 0, 1)

        @pl.when(a_goes_up(zz, r))
        def _():
            a_up(q).wait_send()

        @pl.when(a_goes_down(zz, r))
        def _():
            a_down(q).wait_send()

        @pl.when(own_row & a_crosses(zz))
        def _():
            a_y(q).wait_send()

        @pl.when(own_row & (zz <= z) & (z < 3))
        def _():
            b_up(q, 0).wait_send()
            b_up(q, 1).wait_send()

        @pl.when(own_row & (zz >= z) & (z > 0))
        def _():
            b_down(q, 0).wait_send()
            b_down(q, 1).wait_send()

        @pl.when(q != me)
        def _():
            x_copy(q).wait_send()

        core_copy(q, c).wait_send()
        core_x_copy(q, c).wait_send()
        h_copy(q).wait_send()

        @pl.when(own_row)
        def _():
            b_y(q, 0).wait_send()
            b_y(q, 1).wait_send()

        return carry

    def run(step):
        kind = step // 8
        zz = (step // 2) % 4
        r = step % 2
        q = zz * 2 + jnp.where(r == 0, y, 1 - y)

        def on(k):
            return pl.when(kind == k)

        @pl.when(kind < DOWN)
        def _():
            @on(UP)
            def _():
                core_copy(q, 1 - c).wait_recv()
                core_x_copy(q, 1 - c).wait_recv()
                chunk = lax.broadcasted_iota(jnp.int32, (rows, n_dev), 1)
                for i, s in enumerate((q * 2 + c, q * 2 + 1 - c)):
                    w = jnp.where(chunk == s, wcol[...], 0.0)
                    wblk[q, rows * i:rows * (i + 1)] = jnp.sum(w, axis=1, keepdims=True)

            n = pl.multiple_of(kind * 256, 256)
            a = jnp.concatenate([held[q * 2 + c], held[q * 2 + 1 - c]], axis=0)
            g = jnp.dot(a, gate_v[:, pl.ds(n, 256)], preferred_element_type=F32)
            u = jnp.dot(a, up_v[:, pl.ds(n, 256)], preferred_element_type=F32)
            h = (g / (1.0 + jnp.exp(-g)) * u * wblk[q]).astype(BF16)
            hbuf[q, :, pl.ds(pl.multiple_of(c * units + n, 256), 256)] = h[:rows]
            hsend[q, :, pl.ds(n, 256)] = h[rows:]

            @on(UP_LAST)
            def _():
                h_copy(q).start()

        @on(DOWN)
        def _():
            h_arrive(q).wait_recv()
            h = hbuf[q]
            for n in range(0, width, 512):
                p = jnp.dot(h, down_v[:, n:n + 512], preferred_element_type=F32)
                held[sums(q), :, n:n + 512] = p.astype(BF16)

        @pl.when((kind > DOWN) & (kind < SEND_X))
        def _():
            @on(TOK_A)
            def _():
                a_y(q).wait_recv()

                @pl.when(a_goes_up(zz, r))
                def _():
                    a_up(q).start()

                @pl.when(a_goes_down(zz, r))
                def _():
                    a_down(q).start()

                @pl.when((r == 0) & a_crosses(zz))
                def _():
                    a_y(q).start()

                x_copy(q).start()

            @pl.when((kind == TOK_B0) | (kind == TOK_B1))
            def _():
                h = kind - TOK_B0
                b_y(q, h).wait_recv()
                forward_b(q, zz, h)
                b_y(q, h).start()

            @on(TOK_BO)
            def _():
                b_y(q, 0).wait_recv()
                b_y(q, 1).wait_recv()

            @pl.when((kind == TOK_B1) | (kind == TOK_BO))
            def _():
                core_copy(q, c).start()

            @on(TOK_X)
            def _():
                x_arrive(q).wait_recv()
                core_x_copy(q, c).start()

            @pl.when(kind >= OWN0)
            def _():
                forward_b(q, zz, kind - OWN0)

        @pl.when((kind >= SEND_X) & (kind < CHAIN_C))
        def _():
            @on(SEND_X)
            def _():
                sx_copy(q).start()

            @on(SEND_Y)
            def _():
                sy_copy(zz, q).start()

            @on(SUM_X)
            def _():
                sx_copy(q).wait_recv()
                add(q, ra, keep, got_x[q])

            @on(SUM_Y)
            def _():
                sy_copy(zz, q).wait_recv()
                add(q, rb, slice(None), got_y[zz])
                yx_copy(zz, q).start()

            @on(SUM_YX)
            def _():
                yx_copy(zz, q).wait_recv()
                add(q, rb, keep, got_yx[zz])

        def chain(i):
            got, _, _, part_rows = chains[i]

            @pl.when(((zz > z) & (z > 0)) | ((zz < z) & (z < 3)))
            def _():
                chain_arrive(i, zz, q).wait_recv()
                add(q, part_rows, keep, got[zz])

            @pl.when(zz > z)
            def _():
                chain_up(i, zz, q).start()

            @pl.when(zz < z)
            def _():
                chain_down(i, zz, q).start()

        def finish(i):
            got, _, _, part_rows = chains[i]

            @pl.when(z > 0)
            def _():
                chain_arrive(i, z, q).wait_recv()
                add(q, part_rows, keep, got[z])

            @pl.when(z < 3)
            def _():
                chain_arrive(i, 4, q).wait_recv()
                add(q, part_rows, keep, got[4])

        @pl.when(kind >= CHAIN_C)
        def _():
            @on(GOT_W)
            def _():
                lax.fori_loop(1, n_dev, got_w, 0)
                expert = lax.broadcasted_iota(jnp.int32, (n_dev, experts, rows), 1)
                wcol[...] = jnp.sum(jnp.where(expert == e, wall[...], 0.0), axis=1).T
                load_gate.wait()
                load_up.wait()

            @on(DRAIN)
            def _():
                lax.fori_loop(1, n_dev, drain_w, 0)
                down_copy(mine).wait_send()
                lax.fori_loop(0, 8, drain_tokens, 0)

            @on(GOT_DOWN)
            def _():
                load_down.wait()
                down_copy(theirs).wait_recv()

            for i, k in enumerate((CHAIN_C, CHAIN_O, CHAIN_B)):
                @on(k)
                def _():
                    chain(i)

            @on(END_O)
            def _():
                finish(1)
                end_copy(q).start()

            @on(END_C)
            def _():
                finish(0)
                end_copy(q).wait_recv()
                add(q, ra, keep, got_end[...])
                out[ra] = held[sums(q), ra, keep]

            @on(END_B)
            def _():
                finish(2)
                out[rb] = held[sums(q), rb, keep]

    def steps(i, carry):
        word = word_at(z, i)

        def one(k, rest):
            run(rest % BASE)
            return rest // BASE

        lax.fori_loop(0, 4, one, word)
        return carry

    lax.fori_loop(0, len(WORDS[0]), steps, 0)

    def drain(q, carry):
        zz = q // 2
        own_row = q % 2 == y

        sx_copy(q).wait_send()

        @pl.when(own_row)
        def _():
            yx_copy(zz, q).wait_send()

        @pl.when(~own_row)
        def _():
            sy_copy(zz, q).wait_send()

        for i in range(3):
            @pl.when((own_row if i != 1 else ~own_row) & (zz > z))
            def _():
                chain_up(i, zz, q).wait_send()

            @pl.when((own_row if i != 1 else ~own_row) & (zz < z))
            def _():
                chain_down(i, zz, q).wait_send()

        return carry

    lax.fori_loop(0, 8, drain, 0)
    end_copy(z * 2 + 1 - y).wait_send()


def dense_weights(expert_ids, route_weights, experts):
    hit = expert_ids[None] == jnp.arange(experts, dtype=jnp.int32)[:, None, None]
    return jnp.sum(jnp.where(hit, route_weights[None], 0.0), axis=2)


def on_box(tokens, expert_ids, route_weights, gate_w, up_w, down_w):
    rows, width = tokens.shape
    n_dev = lax.axis_size("expert")
    units = gate_w.shape[2]
    any_ = pl.BlockSpec(memory_space=pl.ANY)
    vmem = pl.BlockSpec(memory_space=pltpu.VMEM)
    sem = lambda *s: pltpu.SemaphoreType.DMA(s)
    buf = lambda *s: pltpu.VMEM(s, BF16)
    half = width // 2
    top = TOP
    low = rows - top
    return pl.pallas_call(
        layer_kernel,
        out_shape=jax.ShapeDtypeStruct((rows, half), BF16),
        in_specs=[any_] * 6,
        out_specs=vmem,
        scratch_shapes=[
            buf(n_dev, rows, width), buf(width, units), buf(width, units), buf(2 * units, width),
            pltpu.VMEM((n_dev, n_dev, rows), F32), pltpu.VMEM((rows, n_dev), F32),
            pltpu.VMEM((8, 2 * rows, 1), F32), pltpu.VMEM(expert_ids.shape[::-1], jnp.int32),
            pltpu.VMEM(route_weights.shape[::-1], F32),
            buf(8, rows, 2 * units), buf(8, rows, units),
            buf(8, top, half), buf(4, low, width), buf(4, low, half),
            buf(5, top, half), buf(5, top, half), buf(5, low, half), buf(top, half),
            sem(6), sem(n_dev), sem(n_dev), sem(2, 8), sem(2, 4, 2), sem(4), sem(4, 2), sem(8),
            sem(8), sem(8), sem(8), sem(1),
            sem(8), sem(8, 2), sem(8), sem(8), sem(8), sem(8), sem(1),
            sem(8), sem(8), sem(4), sem(4), sem(4), sem(4),
            sem(4), sem(5), sem(4), sem(5), sem(4), sem(5), sem(1), sem(1),
        ],
        compiler_params=pltpu.CompilerParams(
            collective_id=0, has_side_effects=True, vmem_limit_bytes=62 * 2**20
        ),
        name="moe_layer",
    )(tokens, expert_ids.T, route_weights.T, gate_w, up_w, down_w)


def anywhere(tokens, expert_ids, route_weights, gate_w, up_w, down_w):
    rows, width = tokens.shape
    local_experts = gate_w.shape[0]
    experts = local_experts * lax.axis_size("expert")
    first = lax.axis_index("expert") * local_experts
    wts = dense_weights(expert_ids, route_weights, experts)
    every = lax.all_gather(tokens, "expert", axis=0, tiled=True)
    wall = lax.all_gather(wts, "expert", axis=1, tiled=True)
    total = None
    for i in range(local_experts):
        w = lax.dynamic_index_in_dim(wall, first + i, 0, keepdims=False)[:, None]
        g = jnp.dot(every, gate_w[i], preferred_element_type=F32)
        u = jnp.dot(every, up_w[i], preferred_element_type=F32)
        h = (jax.nn.silu(g) * u * w).astype(BF16)
        p = jnp.dot(h, down_w[i], preferred_element_type=F32)
        total = p if total is None else total + p
    mixed = lax.psum_scatter(total.astype(BF16), "expert", scatter_dimension=0, tiled=True)
    return lax.psum_scatter(mixed, "tensor", scatter_dimension=1, tiled=True)


def solution(mesh):
    shape = dict(mesh.shape)
    box = shape == {"groups": 1, "expert": 16, "tensor": 2}
    in_specs = (
        P(("groups", "expert"), None),
        P(("groups", "expert"), None),
        P(("groups", "expert"), None),
        P("expert", None, "tensor"),
        P("expert", None, "tensor"),
        P("expert", "tensor", None),
    )
    out_specs = P(("groups", "expert"), "tensor")
    return jax.shard_map(
        on_box if box else anywhere, mesh=mesh, in_specs=in_specs, out_specs=out_specs, check_vma=False
    )
```

```python
import jax
import jax.numpy as jnp
from jax import lax
from jax.experimental import pallas as pl
from jax.experimental.pallas import tpu as pltpu
from jax.sharding import PartitionSpec as P

MESH = pl.DeviceIdType.MESH
F32, BF16 = jnp.float32, jnp.bfloat16
BASE = 215
TOP = 64
FAR = 2
(UP, UP_LAST, DOWN, TOK_A, TOK_B0, TOK_B1, TOK_BO, TOK_X, OWN0, OWN1, SEND_X, SEND_Y, SUM_X, SUM_Y, SUM_YX, SUM_YX1,
 CHAIN_C, CHAIN_O, CHAIN_B, CHAIN_B1, END_O, END_C, END_B, END_B1, OTHER) = (0,) + tuple(range(2, 26))
WORDS = (
    (
        9262272, 329541473, 360837712, 11570282, 677569714, 420514237, 22203089, 686589825,
        537886873, 113483091, 61686529, 627384849, 1376406802, 1044917721, 934783239, 1064112635,
        915629892, 1028744045, 213100187, 925639608, 1139976551, 1178399844, 1259744685, 1655998486,
        1636028864, 1539963899, 1280287280, 2056872082,
    ),
    (
        179353630, 2009177397, 380625276, 370873554, 327984079, 161154763, 696807908, 60510944,
        219306279, 648403970, 10143515, 94044479, 199335332, 53765160, 967308878, 291144858,
        153191259, 312781593, 1027974220, 1089871446, 1298479937, 1070411606, 1338654841, 1575467255,
        1200315247, 1281575592, 1856801220, 2056872084,
    ),
    (
        199323260, 2009269423, 697175368, 350905646, 387892111, 220508099, 637456300, 973568,
        159398247, 707942202, 69680019, 153767603, 179365708, 34167044, 1026661346, 270990326,
        93837075, 253058457, 968252804, 1069717770, 1318264669, 1090009722, 1278931705, 1516113931,
        1259668575, 1341205418, 1876769996, 2056872086,
    ),
    (
        68893818, 389265469, 341054702, 71294278, 657416910, 440484725, 42170993, 666804237,
        478349509, 133452715, 1965121, 567848333, 1396375566, 1104269333, 875060967, 1083711603,
        895659404, 968835153, 192945651, 905669976, 1159575515, 1118861612, 1200208177, 1596089594,
        1616059232, 1559841945, 1340196176, 2056872088,
    ),
)


def place():
    e = lax.axis_index("expert")
    return e, e // 4, (e // 2) % 2, e % 2, lax.axis_index("tensor")


def dev(z, y, c, x):
    return {"expert": (z * 2 + y) * 2 + c, "tensor": x}


def word_at(z, i):
    out = jnp.int32(0)
    for k, column in enumerate(zip(*WORDS)):
        w = jnp.int32(column[3])
        for zz in range(3):
            w = jnp.where(z == zz, jnp.int32(column[zz]), w)
        out = jnp.where(i == k, w, out)
    return out


def layer_kernel(
    tok, ids_hbm, route_hbm, gate_hbm, up_hbm, down_hbm, out,
    held, gate_v, up_v, down_v, wall, wcol, wblk, ids_v, route_v, hbuf, hsend, got_x, got_y, got_yx, got_c, got_o, got_b, got_d, got_end,
    load_s, wsend, wrecv, za_s, zb_s, ya_s, yb_s, x_s, ca_s, cb_s, h_s, dn_s,
    a_r, b_r, x_r, ca_r, cb_r, h_r, dn_r,
    sx_s, sx_r, sy_s, sy_r, yx_s, yx_r, kc_s, kc_r, ko_s, ko_r, kb_s, kb_r, kd_s, kd_r, en_s, en_r,
):
    e, z, y, c, x = place()
    n_dev = wall.shape[0]
    rows, width = held.shape[1], held.shape[2]
    units = gate_v.shape[1]
    part = rows // 4
    top = got_x.shape[1]
    half = width // 2
    above, below = dev(jnp.minimum(z + 1, 3), y, c, x), dev(jnp.maximum(z - 1, 0), y, c, x)
    peer_c, peer_x, peer_y = dev(z, y, 1 - c, x), dev(z, y, c, 1 - x), dev(z, 1 - y, c, x)
    keep = pl.ds(pl.multiple_of(x * half, 128), half)
    give = pl.ds(pl.multiple_of((1 - x) * half, 128), half)
    ra, rb = pl.ds(0, top), pl.ds(top, rows - top)
    low = (rows - top) // 2
    rbs = pl.ds(top, low), pl.ds(top + low, low)
    rows_a = pl.ds(pl.multiple_of(x * (rows - part), 16), part)
    rows_x = pl.ds(pl.multiple_of((1 - x) * (rows - part), 16), part)
    rows_main = pl.ds(pl.multiple_of(x * part, 16), rows - part)

    def rcopy(src, dst, send, recv, target):
        return pltpu.make_async_remote_copy(
            src_ref=src, dst_ref=dst, send_sem=send, recv_sem=recv, device_id=target, device_id_type=MESH
        )

    load_own = pltpu.make_async_copy(tok, held.at[e], load_s.at[0])
    load_ids = pltpu.make_async_copy(ids_hbm, ids_v, load_s.at[1])
    load_route = pltpu.make_async_copy(route_hbm, route_v, load_s.at[5])
    load_gate = pltpu.make_async_copy(gate_hbm.at[0], gate_v, load_s.at[2])
    load_up = pltpu.make_async_copy(up_hbm.at[0], up_v, load_s.at[3])
    mine = pl.ds(pl.multiple_of(c * units, 128), units)
    theirs = pl.ds(pl.multiple_of((1 - c) * units, 128), units)
    load_down = pltpu.make_async_copy(down_hbm.at[0], down_v.at[mine], load_s.at[4])
    load_own.start()
    load_ids.start()
    load_route.start()
    load_gate.start()
    load_up.start()
    load_down.start()

    barrier = pltpu.get_barrier_semaphore()

    def greet(k, carry):
        pl.semaphore_signal(
            barrier, inc=1, device_id={"expert": (e + k) % n_dev, "tensor": x}, device_id_type=MESH
        )
        return carry

    lax.fori_loop(1, n_dev, greet, 0)
    pl.semaphore_signal(barrier, inc=1, device_id=peer_x, device_id_type=MESH)
    load_ids.wait()
    load_route.wait()
    experts = wall.shape[1]
    expert = lax.broadcasted_iota(jnp.int32, (experts, rows), 0)
    dense = jnp.zeros((experts, rows), F32)
    for k in range(ids_v.shape[0]):
        dense = dense + jnp.where(ids_v[k:k + 1] == expert, route_v[k:k + 1], 0.0)
    wall[e] = dense
    pl.semaphore_wait(barrier, n_dev)

    def tok_copy(q, part_rows, send, recv, target):
        ref = held.at[q * 2 + c, part_rows]
        return rcopy(ref, ref, send, recv, target)

    def b_rows(h):
        return pl.ds(part * (1 + h), part)

    def a_up(q):
        return tok_copy(q, rows_a, za_s.at[0, q], a_r.at[q], above)

    def a_down(q):
        return tok_copy(q, rows_a, za_s.at[1, q], a_r.at[q], below)

    def a_y(q):
        return tok_copy(q, rows_a, ya_s.at[q // 2], a_r.at[q], peer_y)

    def a_goes_up(zz, r):
        return (zz <= z) & (z < 3) & ((r == 0) | (z < 2) | (zz > 3 - FAR))

    def a_goes_down(zz, r):
        return (zz >= z) & (z > 0) & ((r == 0) | (z > 1) | (zz < FAR))

    def a_crosses(zz):
        return ((z == 0) & (zz >= FAR)) | ((z == 3) & (zz <= 3 - FAR)) | (zz == z)

    def b_up(q, h):
        return tok_copy(q, b_rows(h), zb_s.at[0, q // 2, h], b_r.at[q, h], above)

    def b_down(q, h):
        return tok_copy(q, b_rows(h), zb_s.at[1, q // 2, h], b_r.at[q, h], below)

    def b_y(q, h):
        return tok_copy(q, b_rows(h), yb_s.at[q // 2, h], b_r.at[q, h], peer_y)

    def x_copy(q):
        return tok_copy(q, rows_a, x_s.at[q], x_r.at[q], peer_x)

    def x_arrive(q):
        return tok_copy(q, rows_x, x_s.at[q], x_r.at[q], peer_x)

    def core_copy(q, lane):
        ref = held.at[q * 2 + lane, rows_main]
        return rcopy(ref, ref, ca_s.at[q], ca_r.at[q], peer_c)

    def core_x_copy(q, lane):
        ref = held.at[q * 2 + lane, rows_x]
        return rcopy(ref, ref, cb_s.at[q], cb_r.at[q], peer_c)

    def h_copy(q):
        return rcopy(hsend.at[q], hbuf.at[q, :, mine], h_s.at[q], h_r.at[q], peer_c)

    def h_arrive(q):
        return rcopy(hsend.at[q], hbuf.at[q, :, theirs], h_s.at[q], h_r.at[q], peer_c)

    def down_copy(where):
        return rcopy(down_hbm.at[0], down_v.at[where], dn_s.at[0], dn_r.at[0], peer_c)

    def w_copy(k):
        return rcopy(
            wall.at[e], wall.at[e], wsend.at[k], wrecv.at[k], {"expert": (e + k) % n_dev, "tensor": x}
        )

    def w_arrive(k):
        ref = wall.at[(e + n_dev - k) % n_dev]
        return rcopy(ref, ref, wsend.at[k], wrecv.at[k], {"expert": (e + k) % n_dev, "tensor": x})

    def sums(q):
        return q * 2 + 1 - c

    def sx_copy(q):
        return rcopy(held.at[sums(q), ra, give], got_x.at[q], sx_s.at[q], sx_r.at[q], peer_x)

    def sy_copy(t, q):
        return rcopy(held.at[sums(q), rb], got_y.at[t], sy_s.at[t], sy_r.at[t], peer_y)

    def yx_copy(t, q, i):
        return rcopy(held.at[sums(q), rbs[i], give], got_yx.at[i, t], yx_s.at[i, t], yx_r.at[i, t], peer_x)

    def end_copy(q):
        return rcopy(held.at[sums(q), ra, keep], got_end, en_s.at[0], en_r.at[0], peer_y)

    chains = ((got_c, kc_s, kc_r, ra), (got_o, ko_s, ko_r, ra), (got_b, kb_s, kb_r, rbs[0]),
              (got_d, kd_s, kd_r, rbs[1]))

    def chain_up(kind, t, q):
        got, s, r, part_rows = chains[kind]
        return rcopy(held.at[sums(q), part_rows, keep], got.at[t], s.at[t], r.at[t], above)

    def chain_down(kind, t, q):
        got, s, r, part_rows = chains[kind]
        slot = jnp.where(t == z - 1, 4, t)
        return rcopy(held.at[sums(q), part_rows, keep], got.at[slot], s.at[t], r.at[slot], below)

    def chain_arrive(kind, slot, q):
        got, s, r, part_rows = chains[kind]
        return rcopy(held.at[sums(q), part_rows, keep], got.at[slot], s.at[0], r.at[slot], below)

    def add(q, r, cols, other):
        s = sums(q)
        held[s, r, cols] = (held[s, r, cols].astype(F32) + other.astype(F32)).astype(BF16)

    me = z * 2 + y
    load_own.wait()

    @pl.when(z < 3)
    def _():
        a_up(me).start()

    @pl.when(z > 0)
    def _():
        a_down(me).start()

    a_y(me).start()
    core_copy(me, c).start()
    core_x_copy(me, c).start()
    b_y(me, 0).start()
    b_y(me, 1).start()
    def send_w(k, carry):
        w_copy(k).start()
        return carry

    lax.fori_loop(1, n_dev, send_w, 0)
    down_copy(mine).start()

    def got_w(k, carry):
        w_arrive(k).wait_recv()
        return carry

    def forward_b(q, zz, h):
        @pl.when((zz <= z) & (z < 3))
        def _():
            b_up(q, h).start()

        @pl.when((zz >= z) & (z > 0))
        def _():
            b_down(q, h).start()

    def drain_w(k, carry):
        w_copy(k).wait_send()
        return carry

    def drain_tokens(q, carry):
        zz = q // 2
        own_row = q % 2 == y

        r = jnp.where(own_row, 0, 1)

        @pl.when(a_goes_up(zz, r))
        def _():
            a_up(q).wait_send()

        @pl.when(a_goes_down(zz, r))
        def _():
            a_down(q).wait_send()

        @pl.when(own_row & a_crosses(zz))
        def _():
            a_y(q).wait_send()

        @pl.when(own_row & (zz <= z) & (z < 3))
        def _():
            b_up(q, 0).wait_send()
            b_up(q, 1).wait_send()

        @pl.when(own_row & (zz >= z) & (z > 0))
        def _():
            b_down(q, 0).wait_send()
            b_down(q, 1).wait_send()

        @pl.when(q != me)
        def _():
            x_copy(q).wait_send()

        core_copy(q, c).wait_send()
        core_x_copy(q, c).wait_send()
        h_copy(q).wait_send()

        @pl.when(own_row)
        def _():
            b_y(q, 0).wait_send()
            b_y(q, 1).wait_send()

        return carry

    def run(step):
        kind = step // 8
        zz = (step // 2) % 4
        r = step % 2
        q = zz * 2 + jnp.where(r == 0, y, 1 - y)

        def on(k):
            return pl.when(kind == k)

        @pl.when(kind < DOWN)
        def _():
            @on(UP)
            def _():
                core_copy(q, 1 - c).wait_recv()
                core_x_copy(q, 1 - c).wait_recv()
                chunk = lax.broadcasted_iota(jnp.int32, (rows, n_dev), 1)
                for i, s in enumerate((q * 2 + c, q * 2 + 1 - c)):
                    w = jnp.where(chunk == s, wcol[...], 0.0)
                    wblk[q, rows * i:rows * (i + 1)] = jnp.sum(w, axis=1, keepdims=True)

            n = pl.multiple_of(kind * 256, 256)
            a = jnp.concatenate([held[q * 2 + c], held[q * 2 + 1 - c]], axis=0)
            g = jnp.dot(a, gate_v[:, pl.ds(n, 256)], preferred_element_type=F32)
            u = jnp.dot(a, up_v[:, pl.ds(n, 256)], preferred_element_type=F32)
            h = (g / (1.0 + jnp.exp(-g)) * u * wblk[q]).astype(BF16)
            hbuf[q, :, pl.ds(pl.multiple_of(c * units + n, 256), 256)] = h[:rows]
            hsend[q, :, pl.ds(n, 256)] = h[rows:]

            @on(UP_LAST)
            def _():
                h_copy(q).start()

        @on(DOWN)
        def _():
            h_arrive(q).wait_recv()
            h = hbuf[q]
            for n in range(0, width, 512):
                p = jnp.dot(h, down_v[:, n:n + 512], preferred_element_type=F32)
                held[sums(q), :, n:n + 512] = p.astype(BF16)

        @pl.when((kind > DOWN) & (kind < SEND_X))
        def _():
            @on(TOK_A)
            def _():
                a_y(q).wait_recv()

                @pl.when(a_goes_up(zz, r))
                def _():
                    a_up(q).start()

                @pl.when(a_goes_down(zz, r))
                def _():
                    a_down(q).start()

                @pl.when((r == 0) & a_crosses(zz))
                def _():
                    a_y(q).start()

                x_copy(q).start()

            @pl.when((kind == TOK_B0) | (kind == TOK_B1))
            def _():
                h = kind - TOK_B0
                b_y(q, h).wait_recv()
                forward_b(q, zz, h)
                b_y(q, h).start()

            @on(TOK_BO)
            def _():
                b_y(q, 0).wait_recv()
                b_y(q, 1).wait_recv()

            @pl.when((kind == TOK_B1) | (kind == TOK_BO))
            def _():
                core_copy(q, c).start()

            @on(TOK_X)
            def _():
                x_arrive(q).wait_recv()
                core_x_copy(q, c).start()

            @pl.when(kind >= OWN0)
            def _():
                forward_b(q, zz, kind - OWN0)

        @pl.when((kind >= SEND_X) & (kind < CHAIN_C))
        def _():
            @on(SEND_X)
            def _():
                sx_copy(q).start()

            @on(SEND_Y)
            def _():
                sy_copy(zz, q).start()

            @on(SUM_X)
            def _():
                sx_copy(q).wait_recv()
                add(q, ra, keep, got_x[q])

            @on(SUM_Y)
            def _():
                sy_copy(zz, q).wait_recv()
                add(q, rb, slice(None), got_y[zz])
                yx_copy(zz, q, 0).start()
                yx_copy(zz, q, 1).start()

            for i in range(2):
                @on(SUM_YX + i)
                def _():
                    yx_copy(zz, q, i).wait_recv()
                    add(q, rbs[i], keep, got_yx[i, zz])

        def chain(i):
            got, _, _, part_rows = chains[i]

            @pl.when(((zz > z) & (z > 0)) | ((zz < z) & (z < 3)))
            def _():
                chain_arrive(i, zz, q).wait_recv()
                add(q, part_rows, keep, got[zz])

            @pl.when(zz > z)
            def _():
                chain_up(i, zz, q).start()

            @pl.when(zz < z)
            def _():
                chain_down(i, zz, q).start()

        def finish(i):
            got, _, _, part_rows = chains[i]

            @pl.when(z > 0)
            def _():
                chain_arrive(i, z, q).wait_recv()
                add(q, part_rows, keep, got[z])

            @pl.when(z < 3)
            def _():
                chain_arrive(i, 4, q).wait_recv()
                add(q, part_rows, keep, got[4])

        @pl.when(kind >= CHAIN_C)
        def _():
            @pl.when((kind == OTHER) & (zz == 0))
            def _():
                lax.fori_loop(1, n_dev, got_w, 0)
                expert = lax.broadcasted_iota(jnp.int32, (n_dev, experts, rows), 1)
                wcol[...] = jnp.sum(jnp.where(expert == e, wall[...], 0.0), axis=1).T
                load_gate.wait()
                load_up.wait()

            @pl.when((kind == OTHER) & (zz == 2))
            def _():
                lax.fori_loop(1, n_dev, drain_w, 0)
                down_copy(mine).wait_send()
                lax.fori_loop(0, 8, drain_tokens, 0)

            @pl.when((kind == OTHER) & (zz == 1))
            def _():
                load_down.wait()
                down_copy(theirs).wait_recv()

            for i, k in enumerate((CHAIN_C, CHAIN_O, CHAIN_B, CHAIN_B1)):
                @on(k)
                def _():
                    chain(i)

            @on(END_O)
            def _():
                finish(1)
                end_copy(q).start()

            @on(END_C)
            def _():
                finish(0)
                end_copy(q).wait_recv()
                add(q, ra, keep, got_end[...])
                out[ra] = held[sums(q), ra, keep]

            for i in range(2):
                @on(END_B + i)
                def _():
                    finish(2 + i)
                    out[rbs[i]] = held[sums(q), rbs[i], keep]

    def steps(i, carry):
        word = word_at(z, i)

        def one(k, rest):
            run(rest % BASE)
            return rest // BASE

        lax.fori_loop(0, 4, one, word)
        return carry

    lax.fori_loop(0, len(WORDS[0]), steps, 0)

    def drain(q, carry):
        zz = q // 2
        own_row = q % 2 == y

        sx_copy(q).wait_send()

        @pl.when(own_row)
        def _():
            yx_copy(zz, q, 0).wait_send()
            yx_copy(zz, q, 1).wait_send()

        @pl.when(~own_row)
        def _():
            sy_copy(zz, q).wait_send()

        for i in range(4):
            @pl.when((own_row if i != 1 else ~own_row) & (zz > z))
            def _():
                chain_up(i, zz, q).wait_send()

            @pl.when((own_row if i != 1 else ~own_row) & (zz < z))
            def _():
                chain_down(i, zz, q).wait_send()

        return carry

    lax.fori_loop(0, 8, drain, 0)
    end_copy(z * 2 + 1 - y).wait_send()


def dense_weights(expert_ids, route_weights, experts):
    hit = expert_ids[None] == jnp.arange(experts, dtype=jnp.int32)[:, None, None]
    return jnp.sum(jnp.where(hit, route_weights[None], 0.0), axis=2)


def on_box(tokens, expert_ids, route_weights, gate_w, up_w, down_w):
    rows, width = tokens.shape
    n_dev = lax.axis_size("expert")
    units = gate_w.shape[2]
    any_ = pl.BlockSpec(memory_space=pl.ANY)
    vmem = pl.BlockSpec(memory_space=pltpu.VMEM)
    sem = lambda *s: pltpu.SemaphoreType.DMA(s)
    buf = lambda *s: pltpu.VMEM(s, BF16)
    half = width // 2
    top = TOP
    low = rows - top
    return pl.pallas_call(
        layer_kernel,
        out_shape=jax.ShapeDtypeStruct((rows, half), BF16),
        in_specs=[any_] * 6,
        out_specs=vmem,
        scratch_shapes=[
            buf(n_dev, rows, width), buf(width, units), buf(width, units), buf(2 * units, width),
            pltpu.VMEM((n_dev, n_dev, rows), F32), pltpu.VMEM((rows, n_dev), F32),
            pltpu.VMEM((8, 2 * rows, 1), F32), pltpu.VMEM(expert_ids.shape[::-1], jnp.int32),
            pltpu.VMEM(route_weights.shape[::-1], F32),
            buf(8, rows, 2 * units), buf(8, rows, units),
            buf(8, top, half), buf(4, low, width), buf(2, 4, low // 2, half),
            buf(5, top, half), buf(5, top, half), buf(5, low // 2, half), buf(5, low // 2, half), buf(top, half),
            sem(6), sem(n_dev), sem(n_dev), sem(2, 8), sem(2, 4, 2), sem(4), sem(4, 2), sem(8),
            sem(8), sem(8), sem(8), sem(1),
            sem(8), sem(8, 2), sem(8), sem(8), sem(8), sem(8), sem(1),
            sem(8), sem(8), sem(4), sem(4), sem(2, 4), sem(2, 4),
            sem(4), sem(5), sem(4), sem(5), sem(4), sem(5), sem(4), sem(5), sem(1), sem(1),
        ],
        compiler_params=pltpu.CompilerParams(
            collective_id=0, has_side_effects=True, vmem_limit_bytes=62 * 2**20
        ),
        name="moe_layer",
    )(tokens, expert_ids.T, route_weights.T, gate_w, up_w, down_w)


def anywhere(tokens, expert_ids, route_weights, gate_w, up_w, down_w):
    rows, width = tokens.shape
    local_experts = gate_w.shape[0]
    experts = local_experts * lax.axis_size("expert")
    first = lax.axis_index("expert") * local_experts
    wts = dense_weights(expert_ids, route_weights, experts)
    every = lax.all_gather(tokens, "expert", axis=0, tiled=True)
    wall = lax.all_gather(wts, "expert", axis=1, tiled=True)
    total = None
    for i in range(local_experts):
        w = lax.dynamic_index_in_dim(wall, first + i, 0, keepdims=False)[:, None]
        g = jnp.dot(every, gate_w[i], preferred_element_type=F32)
        u = jnp.dot(every, up_w[i], preferred_element_type=F32)
        h = (jax.nn.silu(g) * u * w).astype(BF16)
        p = jnp.dot(h, down_w[i], preferred_element_type=F32)
        total = p if total is None else total + p
    mixed = lax.psum_scatter(total.astype(BF16), "expert", scatter_dimension=0, tiled=True)
    return lax.psum_scatter(mixed, "tensor", scatter_dimension=1, tiled=True)


def solution(mesh):
    shape = dict(mesh.shape)
    box = shape == {"groups": 1, "expert": 16, "tensor": 2}
    in_specs = (
        P(("groups", "expert"), None),
        P(("groups", "expert"), None),
        P(("groups", "expert"), None),
        P("expert", None, "tensor"),
        P("expert", None, "tensor"),
        P("expert", "tensor", None),
    )
    out_specs = P(("groups", "expert"), "tensor")
    return jax.shard_map(
        on_box if box else anywhere, mesh=mesh, in_specs=in_specs, out_specs=out_specs, check_vma=False
    )
```

```python
import jax
import jax.numpy as jnp
from jax import lax
from jax.experimental import pallas as pl
from jax.experimental.pallas import tpu as pltpu
from jax.sharding import PartitionSpec as P

MESH = pl.DeviceIdType.MESH
F32, BF16 = jnp.float32, jnp.bfloat16
BASE = 215
TOP = 64
FAR = 2
(UP, UP_LAST, DOWN, TOK_A, TOK_B0, TOK_B1, TOK_BO, TOK_X, OWN0, OWN1, SEND_X, SEND_Y, SUM_X, SUM_Y, SUM_Y1, SUM_YX, SUM_YX1,
 CHAIN_C, CHAIN_O, CHAIN_B, CHAIN_B1, END_O, END_C, END_B, END_B1, OTHER) = (0,) + tuple(range(2, 27))
WORDS = (
    (
        9632072, 329541473, 350899345, 11616507, 380758989, 420560462, 22203089, 686589825,
        706839248, 113483074, 61686529, 627384849, 1455913802, 1044917721, 934762909, 1064112635,
        915629900, 1495847670, 213100148, 925641328, 1177431271, 1140255636, 1735866274, 1655805827,
        1379105154, 1715896250, 1619844147, 1837935360, 2136750602,
    ),
    (
        179353638, 2088730407, 380625276, 818377779, 327974397, 112475318, 161650564, 241768387,
        139429479, 648402893, 10142655, 986819789, 606799239, 935385685, 211990650, 73827442,
        229299679, 1025108909, 1107481220, 1259194471, 1477093324, 1585872177, 1376880969, 1526606582,
        1240430142, 1280422101, 1401208484, 1936679740, 2136750612,
    ),
    (
        199323268, 2088638393, 697175368, 838348271, 387888845, 132258330, 221559456, 301119999,
        79521447, 707939409, 69680879, 1006417905, 586831335, 876033213, 191836118, 14104318,
        169390787, 965200885, 1047759804, 1199285579, 1456939652, 1526335661, 1396665701, 1586330570,
        1220275618, 1340143517, 1381333022, 1956648516, 2136750614,
    ),
    (
        69263618, 389265469, 370869835, 71155603, 321222485, 440346050, 42170993, 666804237,
        647301884, 133452698, 1965121, 567848333, 1475882566, 1104269333, 875039781, 1083711603,
        895659412, 1435938778, 192945612, 905671696, 1117707275, 1160039500, 1675958238, 1596268463,
        1398889022, 1695928342, 1639722193, 1897844256, 2136750608,
    ),
)


def place():
    e = lax.axis_index("expert")
    return e, e // 4, (e // 2) % 2, e % 2, lax.axis_index("tensor")


def dev(z, y, c, x):
    return {"expert": (z * 2 + y) * 2 + c, "tensor": x}


def word_at(z, i):
    out = jnp.int32(0)
    for k, column in enumerate(zip(*WORDS)):
        w = jnp.int32(column[3])
        for zz in range(3):
            w = jnp.where(z == zz, jnp.int32(column[zz]), w)
        out = jnp.where(i == k, w, out)
    return out


def layer_kernel(
    tok, ids_hbm, route_hbm, gate_hbm, up_hbm, down_hbm, out,
    held, gate_v, up_v, down_v, wall, wcol, wblk, ids_v, route_v, hbuf, hsend, got_x, got_y, got_yx, got_c, got_o, got_b, got_d, got_end,
    load_s, wsend, wrecv, za_s, zb_s, ya_s, yb_s, x_s, ca_s, cb_s, h_s, dn_s,
    a_r, b_r, x_r, ca_r, cb_r, h_r, dn_r,
    sx_s, sx_r, sy_s, sy_r, yx_s, yx_r, kc_s, kc_r, ko_s, ko_r, kb_s, kb_r, kd_s, kd_r, en_s, en_r,
):
    e, z, y, c, x = place()
    n_dev = wall.shape[0]
    rows, width = held.shape[1], held.shape[2]
    units = gate_v.shape[1]
    part = rows // 4
    top = got_x.shape[1]
    half = width // 2
    above, below = dev(jnp.minimum(z + 1, 3), y, c, x), dev(jnp.maximum(z - 1, 0), y, c, x)
    peer_c, peer_x, peer_y = dev(z, y, 1 - c, x), dev(z, y, c, 1 - x), dev(z, 1 - y, c, x)
    keep = pl.ds(pl.multiple_of(x * half, 128), half)
    give = pl.ds(pl.multiple_of((1 - x) * half, 128), half)
    ra, rb = pl.ds(0, top), pl.ds(top, rows - top)
    low = (rows - top) // 2
    rbs = pl.ds(top, low), pl.ds(top + low, low)
    rows_a = pl.ds(pl.multiple_of(x * (rows - part), 16), part)
    rows_x = pl.ds(pl.multiple_of((1 - x) * (rows - part), 16), part)
    rows_main = pl.ds(pl.multiple_of(x * part, 16), rows - part)

    def rcopy(src, dst, send, recv, target):
        return pltpu.make_async_remote_copy(
            src_ref=src, dst_ref=dst, send_sem=send, recv_sem=recv, device_id=target, device_id_type=MESH
        )

    load_own = pltpu.make_async_copy(tok, held.at[e], load_s.at[0])
    load_ids = pltpu.make_async_copy(ids_hbm, ids_v, load_s.at[1])
    load_route = pltpu.make_async_copy(route_hbm, route_v, load_s.at[5])
    load_gate = pltpu.make_async_copy(gate_hbm.at[0], gate_v, load_s.at[2])
    load_up = pltpu.make_async_copy(up_hbm.at[0], up_v, load_s.at[3])
    mine = pl.ds(pl.multiple_of(c * units, 128), units)
    theirs = pl.ds(pl.multiple_of((1 - c) * units, 128), units)
    load_down = pltpu.make_async_copy(down_hbm.at[0], down_v.at[mine], load_s.at[4])
    load_own.start()

    barrier = pltpu.get_barrier_semaphore()

    def greet(k, carry):
        pl.semaphore_signal(
            barrier, inc=1, device_id={"expert": (e + k) % n_dev, "tensor": x}, device_id_type=MESH
        )
        return carry

    lax.fori_loop(1, n_dev, greet, 0)
    pl.semaphore_signal(barrier, inc=1, device_id=peer_x, device_id_type=MESH)
    load_ids.start()
    load_route.start()
    load_gate.start()
    load_up.start()
    load_down.start()
    load_ids.wait()
    load_route.wait()
    experts = wall.shape[1]
    expert = lax.broadcasted_iota(jnp.int32, (experts, rows), 0)
    dense = jnp.zeros((experts, rows), F32)
    for k in range(ids_v.shape[0]):
        dense = dense + jnp.where(ids_v[k:k + 1] == expert, route_v[k:k + 1], 0.0)
    wall[e] = dense
    pl.semaphore_wait(barrier, n_dev)

    def tok_copy(q, part_rows, send, recv, target):
        ref = held.at[q * 2 + c, part_rows]
        return rcopy(ref, ref, send, recv, target)

    def b_rows(h):
        return pl.ds(part * (1 + h), part)

    def a_up(q):
        return tok_copy(q, rows_a, za_s.at[0, q], a_r.at[q], above)

    def a_down(q):
        return tok_copy(q, rows_a, za_s.at[1, q], a_r.at[q], below)

    def a_y(q):
        return tok_copy(q, rows_a, ya_s.at[q // 2], a_r.at[q], peer_y)

    def a_goes_up(zz, r):
        return (zz <= z) & (z < 3) & ((r == 0) | (z < 2) | (zz > 3 - FAR))

    def a_goes_down(zz, r):
        return (zz >= z) & (z > 0) & ((r == 0) | (z > 1) | (zz < FAR))

    def a_crosses(zz):
        return ((z == 0) & (zz >= FAR)) | ((z == 3) & (zz <= 3 - FAR)) | (zz == z)

    def b_up(q, h):
        return tok_copy(q, b_rows(h), zb_s.at[0, q // 2, h], b_r.at[q, h], above)

    def b_down(q, h):
        return tok_copy(q, b_rows(h), zb_s.at[1, q // 2, h], b_r.at[q, h], below)

    def b_y(q, h):
        return tok_copy(q, b_rows(h), yb_s.at[q // 2, h], b_r.at[q, h], peer_y)

    def x_copy(q):
        return tok_copy(q, rows_a, x_s.at[q], x_r.at[q], peer_x)

    def x_arrive(q):
        return tok_copy(q, rows_x, x_s.at[q], x_r.at[q], peer_x)

    def core_copy(q, lane):
        ref = held.at[q * 2 + lane, rows_main]
        return rcopy(ref, ref, ca_s.at[q], ca_r.at[q], peer_c)

    def core_x_copy(q, lane):
        ref = held.at[q * 2 + lane, rows_x]
        return rcopy(ref, ref, cb_s.at[q], cb_r.at[q], peer_c)

    def h_copy(q):
        return rcopy(hsend.at[q], hbuf.at[q, :, mine], h_s.at[q], h_r.at[q], peer_c)

    def h_arrive(q):
        return rcopy(hsend.at[q], hbuf.at[q, :, theirs], h_s.at[q], h_r.at[q], peer_c)

    def down_copy(where):
        return rcopy(down_hbm.at[0], down_v.at[where], dn_s.at[0], dn_r.at[0], peer_c)

    def w_copy(k):
        return rcopy(
            wall.at[e], wall.at[e], wsend.at[k], wrecv.at[k], {"expert": (e + k) % n_dev, "tensor": x}
        )

    def w_arrive(k):
        ref = wall.at[(e + n_dev - k) % n_dev]
        return rcopy(ref, ref, wsend.at[k], wrecv.at[k], {"expert": (e + k) % n_dev, "tensor": x})

    def sums(q):
        return q * 2 + 1 - c

    def sx_copy(q):
        return rcopy(held.at[sums(q), ra, give], got_x.at[q], sx_s.at[q], sx_r.at[q], peer_x)

    def sy_copy(t, q, i):
        return rcopy(held.at[sums(q), rbs[i]], got_y.at[i, t], sy_s.at[i, t], sy_r.at[i, t], peer_y)

    def yx_copy(t, q, i):
        return rcopy(held.at[sums(q), rbs[i], give], got_yx.at[i, t], yx_s.at[i, t], yx_r.at[i, t], peer_x)

    def end_copy(q):
        return rcopy(held.at[sums(q), ra, keep], got_end, en_s.at[0], en_r.at[0], peer_y)

    chains = ((got_c, kc_s, kc_r, ra), (got_o, ko_s, ko_r, ra), (got_b, kb_s, kb_r, rbs[0]),
              (got_d, kd_s, kd_r, rbs[1]))

    def chain_up(kind, t, q):
        got, s, r, part_rows = chains[kind]
        return rcopy(held.at[sums(q), part_rows, keep], got.at[t], s.at[t], r.at[t], above)

    def chain_down(kind, t, q):
        got, s, r, part_rows = chains[kind]
        slot = jnp.where(t == z - 1, 4, t)
        return rcopy(held.at[sums(q), part_rows, keep], got.at[slot], s.at[t], r.at[slot], below)

    def chain_arrive(kind, slot, q):
        got, s, r, part_rows = chains[kind]
        return rcopy(held.at[sums(q), part_rows, keep], got.at[slot], s.at[0], r.at[slot], below)

    def add(q, r, cols, other):
        s = sums(q)
        held[s, r, cols] = (held[s, r, cols].astype(F32) + other.astype(F32)).astype(BF16)

    me = z * 2 + y
    load_own.wait()

    @pl.when(z < 3)
    def _():
        a_up(me).start()

    @pl.when(z > 0)
    def _():
        a_down(me).start()

    a_y(me).start()
    core_copy(me, c).start()
    core_x_copy(me, c).start()
    b_y(me, 0).start()
    b_y(me, 1).start()
    def send_w(k, carry):
        w_copy(k).start()
        return carry

    lax.fori_loop(1, n_dev, send_w, 0)
    down_copy(mine).start()

    def got_w(k, carry):
        w_arrive(k).wait_recv()
        return carry

    def forward_b(q, zz, h):
        @pl.when((zz <= z) & (z < 3))
        def _():
            b_up(q, h).start()

        @pl.when((zz >= z) & (z > 0))
        def _():
            b_down(q, h).start()

    def drain_w(k, carry):
        w_copy(k).wait_send()
        return carry

    def drain_tokens(q, carry):
        zz = q // 2
        own_row = q % 2 == y

        r = jnp.where(own_row, 0, 1)

        @pl.when(a_goes_up(zz, r))
        def _():
            a_up(q).wait_send()

        @pl.when(a_goes_down(zz, r))
        def _():
            a_down(q).wait_send()

        @pl.when(own_row & a_crosses(zz))
        def _():
            a_y(q).wait_send()

        @pl.when(own_row & (zz <= z) & (z < 3))
        def _():
            b_up(q, 0).wait_send()
            b_up(q, 1).wait_send()

        @pl.when(own_row & (zz >= z) & (z > 0))
        def _():
            b_down(q, 0).wait_send()
            b_down(q, 1).wait_send()

        @pl.when(q != me)
        def _():
            x_copy(q).wait_send()

        core_copy(q, c).wait_send()
        core_x_copy(q, c).wait_send()
        h_copy(q).wait_send()

        @pl.when(own_row)
        def _():
            b_y(q, 0).wait_send()
            b_y(q, 1).wait_send()

        return carry

    def run(step):
        kind = step // 8
        zz = (step // 2) % 4
        r = step % 2
        q = zz * 2 + jnp.where(r == 0, y, 1 - y)

        def on(k):
            return pl.when(kind == k)

        @pl.when(kind < DOWN)
        def _():
            @on(UP)
            def _():
                core_copy(q, 1 - c).wait_recv()
                core_x_copy(q, 1 - c).wait_recv()
                chunk = lax.broadcasted_iota(jnp.int32, (rows, n_dev), 1)
                for i, s in enumerate((q * 2 + c, q * 2 + 1 - c)):
                    w = jnp.where(chunk == s, wcol[...], 0.0)
                    wblk[q, rows * i:rows * (i + 1)] = jnp.sum(w, axis=1, keepdims=True)

            n = pl.multiple_of(kind * 256, 256)
            a = jnp.concatenate([held[q * 2 + c], held[q * 2 + 1 - c]], axis=0)
            g = jnp.dot(a, gate_v[:, pl.ds(n, 256)], preferred_element_type=F32)
            u = jnp.dot(a, up_v[:, pl.ds(n, 256)], preferred_element_type=F32)
            h = (g / (1.0 + jnp.exp(-g)) * u * wblk[q]).astype(BF16)
            hbuf[q, :, pl.ds(pl.multiple_of(c * units + n, 256), 256)] = h[:rows]
            hsend[q, :, pl.ds(n, 256)] = h[rows:]

            @on(UP_LAST)
            def _():
                h_copy(q).start()

        @on(DOWN)
        def _():
            h_arrive(q).wait_recv()
            h = hbuf[q]
            for n in range(0, width, 512):
                p = jnp.dot(h, down_v[:, n:n + 512], preferred_element_type=F32)
                held[sums(q), :, n:n + 512] = p.astype(BF16)

        @pl.when((kind > DOWN) & (kind < SEND_X))
        def _():
            @on(TOK_A)
            def _():
                a_y(q).wait_recv()

                @pl.when(a_goes_up(zz, r))
                def _():
                    a_up(q).start()

                @pl.when(a_goes_down(zz, r))
                def _():
                    a_down(q).start()

                @pl.when((r == 0) & a_crosses(zz))
                def _():
                    a_y(q).start()

                x_copy(q).start()

            @pl.when((kind == TOK_B0) | (kind == TOK_B1))
            def _():
                h = kind - TOK_B0
                b_y(q, h).wait_recv()
                forward_b(q, zz, h)
                b_y(q, h).start()

            @on(TOK_BO)
            def _():
                b_y(q, 0).wait_recv()
                b_y(q, 1).wait_recv()

            @pl.when((kind == TOK_B1) | (kind == TOK_BO))
            def _():
                core_copy(q, c).start()

            @on(TOK_X)
            def _():
                x_arrive(q).wait_recv()
                core_x_copy(q, c).start()

            @pl.when(kind >= OWN0)
            def _():
                forward_b(q, zz, kind - OWN0)

        @pl.when((kind >= SEND_X) & (kind < CHAIN_C))
        def _():
            @on(SEND_X)
            def _():
                sx_copy(q).start()

            @on(SEND_Y)
            def _():
                sy_copy(zz, q, 0).start()
                sy_copy(zz, q, 1).start()

            @on(SUM_X)
            def _():
                sx_copy(q).wait_recv()
                add(q, ra, keep, got_x[q])

            for i in range(2):
                @on(SUM_Y + i)
                def _():
                    sy_copy(zz, q, i).wait_recv()
                    add(q, rbs[i], slice(None), got_y[i, zz])
                    yx_copy(zz, q, i).start()

            for i in range(2):
                @on(SUM_YX + i)
                def _():
                    yx_copy(zz, q, i).wait_recv()
                    add(q, rbs[i], keep, got_yx[i, zz])

        def chain(i):
            got, _, _, part_rows = chains[i]

            @pl.when(((zz > z) & (z > 0)) | ((zz < z) & (z < 3)))
            def _():
                chain_arrive(i, zz, q).wait_recv()
                add(q, part_rows, keep, got[zz])

            @pl.when(zz > z)
            def _():
                chain_up(i, zz, q).start()

            @pl.when(zz < z)
            def _():
                chain_down(i, zz, q).start()

        def finish(i):
            got, _, _, part_rows = chains[i]

            @pl.when(z > 0)
            def _():
                chain_arrive(i, z, q).wait_recv()
                add(q, part_rows, keep, got[z])

            @pl.when(z < 3)
            def _():
                chain_arrive(i, 4, q).wait_recv()
                add(q, part_rows, keep, got[4])

        @pl.when(kind >= CHAIN_C)
        def _():
            @pl.when((kind == OTHER) & (zz == 0))
            def _():
                lax.fori_loop(1, n_dev, got_w, 0)
                expert = lax.broadcasted_iota(jnp.int32, (n_dev, experts, rows), 1)
                wcol[...] = jnp.sum(jnp.where(expert == e, wall[...], 0.0), axis=1).T
                load_gate.wait()
                load_up.wait()

            @pl.when((kind == OTHER) & (zz == 2))
            def _():
                lax.fori_loop(1, n_dev, drain_w, 0)
                down_copy(mine).wait_send()
                lax.fori_loop(0, 8, drain_tokens, 0)

            @pl.when((kind == OTHER) & (zz == 1))
            def _():
                load_down.wait()
                down_copy(theirs).wait_recv()

            for i, k in enumerate((CHAIN_C, CHAIN_O, CHAIN_B, CHAIN_B1)):
                @on(k)
                def _():
                    chain(i)

            @on(END_O)
            def _():
                finish(1)
                end_copy(q).start()

            @on(END_C)
            def _():
                finish(0)
                end_copy(q).wait_recv()
                add(q, ra, keep, got_end[...])
                out[ra] = held[sums(q), ra, keep]

            for i in range(2):
                @on(END_B + i)
                def _():
                    finish(2 + i)
                    out[rbs[i]] = held[sums(q), rbs[i], keep]

    def steps(i, carry):
        word = word_at(z, i)

        def one(k, rest):
            run(rest % BASE)
            return rest // BASE

        lax.fori_loop(0, 4, one, word)
        return carry

    lax.fori_loop(0, len(WORDS[0]), steps, 0)

    def drain(q, carry):
        zz = q // 2
        own_row = q % 2 == y

        sx_copy(q).wait_send()

        @pl.when(own_row)
        def _():
            yx_copy(zz, q, 0).wait_send()
            yx_copy(zz, q, 1).wait_send()

        @pl.when(~own_row)
        def _():
            sy_copy(zz, q, 0).wait_send()
            sy_copy(zz, q, 1).wait_send()

        for i in range(4):
            @pl.when((own_row if i != 1 else ~own_row) & (zz > z))
            def _():
                chain_up(i, zz, q).wait_send()

            @pl.when((own_row if i != 1 else ~own_row) & (zz < z))
            def _():
                chain_down(i, zz, q).wait_send()

        return carry

    lax.fori_loop(0, 8, drain, 0)
    end_copy(z * 2 + 1 - y).wait_send()


def dense_weights(expert_ids, route_weights, experts):
    hit = expert_ids[None] == jnp.arange(experts, dtype=jnp.int32)[:, None, None]
    return jnp.sum(jnp.where(hit, route_weights[None], 0.0), axis=2)


def on_box(tokens, expert_ids, route_weights, gate_w, up_w, down_w):
    rows, width = tokens.shape
    n_dev = lax.axis_size("expert")
    units = gate_w.shape[2]
    any_ = pl.BlockSpec(memory_space=pl.ANY)
    vmem = pl.BlockSpec(memory_space=pltpu.VMEM)
    sem = lambda *s: pltpu.SemaphoreType.DMA(s)
    buf = lambda *s: pltpu.VMEM(s, BF16)
    half = width // 2
    top = TOP
    low = rows - top
    return pl.pallas_call(
        layer_kernel,
        out_shape=jax.ShapeDtypeStruct((rows, half), BF16),
        in_specs=[any_] * 6,
        out_specs=vmem,
        scratch_shapes=[
            buf(n_dev, rows, width), buf(width, units), buf(width, units), buf(2 * units, width),
            pltpu.VMEM((n_dev, n_dev, rows), F32), pltpu.VMEM((rows, n_dev), F32),
            pltpu.VMEM((8, 2 * rows, 1), F32), pltpu.VMEM(expert_ids.shape[::-1], jnp.int32),
            pltpu.VMEM(route_weights.shape[::-1], F32),
            buf(8, rows, 2 * units), buf(8, rows, units),
            buf(8, top, half), buf(2, 4, low // 2, width), buf(2, 4, low // 2, half),
            buf(5, top, half), buf(5, top, half), buf(5, low // 2, half), buf(5, low // 2, half), buf(top, half),
            sem(6), sem(n_dev), sem(n_dev), sem(2, 8), sem(2, 4, 2), sem(4), sem(4, 2), sem(8),
            sem(8), sem(8), sem(8), sem(1),
            sem(8), sem(8, 2), sem(8), sem(8), sem(8), sem(8), sem(1),
            sem(8), sem(8), sem(2, 4), sem(2, 4), sem(2, 4), sem(2, 4),
            sem(4), sem(5), sem(4), sem(5), sem(4), sem(5), sem(4), sem(5), sem(1), sem(1),
        ],
        compiler_params=pltpu.CompilerParams(
            collective_id=0, has_side_effects=True, vmem_limit_bytes=62 * 2**20
        ),
        name="moe_layer",
    )(tokens, expert_ids.T, route_weights.T, gate_w, up_w, down_w)


def anywhere(tokens, expert_ids, route_weights, gate_w, up_w, down_w):
    rows, width = tokens.shape
    local_experts = gate_w.shape[0]
    experts = local_experts * lax.axis_size("expert")
    first = lax.axis_index("expert") * local_experts
    wts = dense_weights(expert_ids, route_weights, experts)
    every = lax.all_gather(tokens, "expert", axis=0, tiled=True)
    wall = lax.all_gather(wts, "expert", axis=1, tiled=True)
    total = None
    for i in range(local_experts):
        w = lax.dynamic_index_in_dim(wall, first + i, 0, keepdims=False)[:, None]
        g = jnp.dot(every, gate_w[i], preferred_element_type=F32)
        u = jnp.dot(every, up_w[i], preferred_element_type=F32)
        h = (jax.nn.silu(g) * u * w).astype(BF16)
        p = jnp.dot(h, down_w[i], preferred_element_type=F32)
        total = p if total is None else total + p
    mixed = lax.psum_scatter(total.astype(BF16), "expert", scatter_dimension=0, tiled=True)
    return lax.psum_scatter(mixed, "tensor", scatter_dimension=1, tiled=True)


def solution(mesh):
    shape = dict(mesh.shape)
    box = shape == {"groups": 1, "expert": 16, "tensor": 2}
    in_specs = (
        P(("groups", "expert"), None),
        P(("groups", "expert"), None),
        P(("groups", "expert"), None),
        P("expert", None, "tensor"),
        P("expert", None, "tensor"),
        P("expert", "tensor", None),
    )
    out_specs = P(("groups", "expert"), "tensor")
    return jax.shard_map(
        on_box if box else anywhere, mesh=mesh, in_specs=in_specs, out_specs=out_specs, check_vma=False
    )
```

```python
import jax
import jax.numpy as jnp
from jax import lax
from jax.experimental import pallas as pl
from jax.experimental.pallas import tpu as pltpu
from jax.sharding import PartitionSpec as P

MESH = pl.DeviceIdType.MESH
F32, BF16 = jnp.float32, jnp.bfloat16
BASE = 215
TOP = 64
FAR = 2
(UP, UP_LAST, DOWN, TOK_A, TOK_B0, TOK_B1, TOK_BO, TOK_X, OWN0, OWN1, SEND_X, SEND_Y, SUM_X, SUM_Y, SUM_Y1, SUM_YX, SUM_YX1,
 CHAIN_C, CHAIN_O, CHAIN_B, CHAIN_B1, END_O, END_C, END_B, END_B1, OTHER) = (0,) + tuple(range(2, 27))
WORDS = (
    (
        9632072, 329541473, 350899345, 11616507, 667631339, 420560462, 22203089, 460358655,
        706839248, 113483074, 442097209, 219911474, 1455913843, 1043859491, 988246859, 1066229095,
        915629900, 1495847670, 213119408, 925641328, 1177431271, 1339024194, 1655160426, 1734947327,
        1379103442, 1715896250, 1281946707, 1834989000, 2136750610,
    ),
    (
        179353638, 2088730407, 380625276, 818377779, 327974397, 80387643, 460312047, 241768387,
        139429479, 648402893, 10142655, 92366039, 203346372, 610591506, 129445293, 229277597,
        968233475, 949144191, 1107295902, 1008661843, 1257305713, 1585870029, 1159255202, 1525776682,
        1279811282, 1359700759, 1401207620, 1936679748, 2136750612,
    ),
    (
        199323268, 2088638393, 697175368, 838348271, 387888845, 140110775, 400590643, 301119999,
        79521447, 707939409, 69680879, 151717655, 183561648, 590438698, 109474801, 169368705,
        1027955739, 889421055, 1047941714, 989061151, 1197582577, 1526330945, 1139471326, 1585684710,
        1339165470, 1419054087, 1381330446, 1956648524, 2136750614,
    ),
    (
        69263618, 389265469, 370869835, 71155603, 687232035, 440346050, 42170993, 400636387,
        647301884, 133452698, 422496521, 160374958, 1475882607, 1103211103, 1007845827, 1086012103,
        895659412, 1435938778, 192964016, 905671696, 1117707275, 1279301922, 1595438150, 1675408243,
        1398887310, 1695928342, 1341577393, 1894897896, 2136750616,
    ),
)


def place():
    e = lax.axis_index("expert")
    return e, e // 4, (e // 2) % 2, e % 2, lax.axis_index("tensor")


def dev(z, y, c, x):
    return {"expert": (z * 2 + y) * 2 + c, "tensor": x}


def word_at(z, i):
    out = jnp.int32(0)
    for k, column in enumerate(zip(*WORDS)):
        w = jnp.int32(column[3])
        for zz in range(3):
            w = jnp.where(z == zz, jnp.int32(column[zz]), w)
        out = jnp.where(i == k, w, out)
    return out


def layer_kernel(
    tok, ids_hbm, route_hbm, gate_hbm, up_hbm, down_hbm, out,
    held, gate_v, up_v, down_v, wall, wcol, wblk, ids_v, route_v, hbuf, hsend, got_x, got_y, got_yx, got_c, got_o, got_b, got_d, got_end,
    load_s, wsend, wrecv, za_s, zb_s, ya_s, yb_s, x_s, ca_s, cb_s, h_s, dn_s,
    a_r, b_r, x_r, ca_r, cb_r, h_r, dn_r,
    sx_s, sx_r, sy_s, sy_r, yx_s, yx_r, kc_s, kc_r, ko_s, ko_r, kb_s, kb_r, kd_s, kd_r, en_s, en_r,
):
    e, z, y, c, x = place()
    n_dev = wall.shape[0]
    rows, width = held.shape[1], held.shape[2]
    units = gate_v.shape[1]
    part = rows // 4
    top = got_x.shape[1]
    half = width // 2
    above, below = dev(jnp.minimum(z + 1, 3), y, c, x), dev(jnp.maximum(z - 1, 0), y, c, x)
    peer_c, peer_x, peer_y = dev(z, y, 1 - c, x), dev(z, y, c, 1 - x), dev(z, 1 - y, c, x)
    keep = pl.ds(pl.multiple_of(x * half, 128), half)
    give = pl.ds(pl.multiple_of((1 - x) * half, 128), half)
    ra, rb = pl.ds(0, top), pl.ds(top, rows - top)
    low = (rows - top) // 2
    rbs = pl.ds(top, low), pl.ds(top + low, low)
    rows_a = pl.ds(pl.multiple_of(x * (rows - part), 16), part)
    rows_x = pl.ds(pl.multiple_of((1 - x) * (rows - part), 16), part)
    rows_main = pl.ds(pl.multiple_of(x * part, 16), rows - part)

    def rcopy(src, dst, send, recv, target):
        return pltpu.make_async_remote_copy(
            src_ref=src, dst_ref=dst, send_sem=send, recv_sem=recv, device_id=target, device_id_type=MESH
        )

    load_own = pltpu.make_async_copy(tok, held.at[e], load_s.at[0])
    load_ids = pltpu.make_async_copy(ids_hbm, ids_v, load_s.at[1])
    load_route = pltpu.make_async_copy(route_hbm, route_v, load_s.at[5])
    load_gate = pltpu.make_async_copy(gate_hbm.at[0], gate_v, load_s.at[2])
    load_up = pltpu.make_async_copy(up_hbm.at[0], up_v, load_s.at[3])
    mine = pl.ds(pl.multiple_of(c * units, 128), units)
    theirs = pl.ds(pl.multiple_of((1 - c) * units, 128), units)
    load_down = pltpu.make_async_copy(down_hbm.at[0], down_v.at[mine], load_s.at[4])
    load_own.start()

    barrier = pltpu.get_barrier_semaphore()

    def greet(k, carry):
        pl.semaphore_signal(
            barrier, inc=1, device_id={"expert": (e + k) % n_dev, "tensor": x}, device_id_type=MESH
        )
        return carry

    lax.fori_loop(1, n_dev, greet, 0)
    pl.semaphore_signal(barrier, inc=1, device_id=peer_x, device_id_type=MESH)
    load_ids.start()
    load_route.start()
    load_gate.start()
    load_up.start()
    load_down.start()
    load_ids.wait()
    load_route.wait()
    experts = wall.shape[1]
    expert = lax.broadcasted_iota(jnp.int32, (experts, rows), 0)
    dense = jnp.zeros((experts, rows), F32)
    for k in range(ids_v.shape[0]):
        dense = dense + jnp.where(ids_v[k:k + 1] == expert, route_v[k:k + 1], 0.0)
    wall[e] = dense
    pl.semaphore_wait(barrier, n_dev)

    def tok_copy(q, part_rows, send, recv, target):
        ref = held.at[q * 2 + c, part_rows]
        return rcopy(ref, ref, send, recv, target)

    def b_rows(h):
        return pl.ds(part * (1 + h), part)

    def a_up(q):
        return tok_copy(q, rows_a, za_s.at[0, q], a_r.at[q], above)

    def a_down(q):
        return tok_copy(q, rows_a, za_s.at[1, q], a_r.at[q], below)

    def a_y(q):
        return tok_copy(q, rows_a, ya_s.at[q // 2], a_r.at[q], peer_y)

    def a_goes_up(zz, r):
        return (zz <= z) & (z < 3) & ((r == 0) | (z < 2) | (zz > 3 - FAR))

    def a_goes_down(zz, r):
        return (zz >= z) & (z > 0) & ((r == 0) | (z > 1) | (zz < FAR))

    def a_crosses(zz):
        return ((z == 0) & (zz >= FAR)) | ((z == 3) & (zz <= 3 - FAR)) | (zz == z)

    def b_up(q, h):
        return tok_copy(q, b_rows(h), zb_s.at[0, q // 2, h], b_r.at[q, h], above)

    def b_down(q, h):
        return tok_copy(q, b_rows(h), zb_s.at[1, q // 2, h], b_r.at[q, h], below)

    def b_y(q, h):
        return tok_copy(q, b_rows(h), yb_s.at[q // 2, h], b_r.at[q, h], peer_y)

    def x_copy(q):
        return tok_copy(q, rows_a, x_s.at[q], x_r.at[q], peer_x)

    def x_arrive(q):
        return tok_copy(q, rows_x, x_s.at[q], x_r.at[q], peer_x)

    def core_copy(q, lane):
        ref = held.at[q * 2 + lane, rows_main]
        return rcopy(ref, ref, ca_s.at[q], ca_r.at[q], peer_c)

    def core_x_copy(q, lane):
        ref = held.at[q * 2 + lane, rows_x]
        return rcopy(ref, ref, cb_s.at[q], cb_r.at[q], peer_c)

    def h_copy(q):
        return rcopy(hsend.at[q], hbuf.at[q, :, mine], h_s.at[q], h_r.at[q], peer_c)

    def h_arrive(q):
        return rcopy(hsend.at[q], hbuf.at[q, :, theirs], h_s.at[q], h_r.at[q], peer_c)

    def down_copy(where):
        return rcopy(down_hbm.at[0], down_v.at[where], dn_s.at[0], dn_r.at[0], peer_c)

    def w_copy(k):
        return rcopy(
            wall.at[e], wall.at[e], wsend.at[k], wrecv.at[k], {"expert": (e + k) % n_dev, "tensor": x}
        )

    def w_arrive(k):
        ref = wall.at[(e + n_dev - k) % n_dev]
        return rcopy(ref, ref, wsend.at[k], wrecv.at[k], {"expert": (e + k) % n_dev, "tensor": x})

    def sums(q):
        return q * 2 + 1 - c

    def sx_copy(q):
        return rcopy(held.at[sums(q), ra, give], got_x.at[q], sx_s.at[q], sx_r.at[q], peer_x)

    def sy_copy(t, q, i):
        return rcopy(held.at[sums(q), rbs[i]], got_y.at[i, t], sy_s.at[i, t], sy_r.at[i, t], peer_y)

    def yx_copy(t, q, i):
        return rcopy(held.at[sums(q), rbs[i], give], got_yx.at[i, t], yx_s.at[i, t], yx_r.at[i, t], peer_x)

    def end_copy(q):
        return rcopy(held.at[sums(q), ra, keep], got_end, en_s.at[0], en_r.at[0], peer_y)

    chains = ((got_c, kc_s, kc_r, ra), (got_o, ko_s, ko_r, ra), (got_b, kb_s, kb_r, rbs[0]),
              (got_d, kd_s, kd_r, rbs[1]))

    def chain_up(kind, t, q):
        got, s, r, part_rows = chains[kind]
        return rcopy(held.at[sums(q), part_rows, keep], got.at[t], s.at[t], r.at[t], above)

    def chain_down(kind, t, q):
        got, s, r, part_rows = chains[kind]
        slot = jnp.where(t == z - 1, 4, t)
        return rcopy(held.at[sums(q), part_rows, keep], got.at[slot], s.at[t], r.at[slot], below)

    def chain_arrive(kind, slot, q):
        got, s, r, part_rows = chains[kind]
        return rcopy(held.at[sums(q), part_rows, keep], got.at[slot], s.at[0], r.at[slot], below)

    def add(q, r, cols, other):
        s = sums(q)
        held[s, r, cols] = (held[s, r, cols].astype(F32) + other.astype(F32)).astype(BF16)

    me = z * 2 + y
    load_own.wait()

    @pl.when(z < 3)
    def _():
        a_up(me).start()

    @pl.when(z > 0)
    def _():
        a_down(me).start()

    a_y(me).start()
    core_copy(me, c).start()
    core_x_copy(me, c).start()
    b_y(me, 0).start()
    b_y(me, 1).start()
    def send_w(k, carry):
        w_copy(k).start()
        return carry

    lax.fori_loop(1, n_dev, send_w, 0)
    down_copy(mine).start()

    def got_w(k, carry):
        w_arrive(k).wait_recv()
        return carry

    def forward_b(q, zz, h):
        @pl.when((zz <= z) & (z < 3))
        def _():
            b_up(q, h).start()

        @pl.when((zz >= z) & (z > 0))
        def _():
            b_down(q, h).start()

    def drain_w(k, carry):
        w_copy(k).wait_send()
        return carry

    def drain_tokens(q, carry):
        zz = q // 2
        own_row = q % 2 == y

        r = jnp.where(own_row, 0, 1)

        @pl.when(a_goes_up(zz, r))
        def _():
            a_up(q).wait_send()

        @pl.when(a_goes_down(zz, r))
        def _():
            a_down(q).wait_send()

        @pl.when(own_row & a_crosses(zz))
        def _():
            a_y(q).wait_send()

        @pl.when(own_row & (zz <= z) & (z < 3))
        def _():
            b_up(q, 0).wait_send()
            b_up(q, 1).wait_send()

        @pl.when(own_row & (zz >= z) & (z > 0))
        def _():
            b_down(q, 0).wait_send()
            b_down(q, 1).wait_send()

        @pl.when(q != me)
        def _():
            x_copy(q).wait_send()

        core_copy(q, c).wait_send()
        core_x_copy(q, c).wait_send()
        h_copy(q).wait_send()

        @pl.when(own_row)
        def _():
            b_y(q, 0).wait_send()
            b_y(q, 1).wait_send()

        return carry

    def run(step):
        kind = step // 8
        zz = (step // 2) % 4
        r = step % 2
        q = zz * 2 + jnp.where(r == 0, y, 1 - y)

        def on(k):
            return pl.when(kind == k)

        @pl.when(kind < DOWN)
        def _():
            @on(UP)
            def _():
                core_copy(q, 1 - c).wait_recv()
                core_x_copy(q, 1 - c).wait_recv()
                chunk = lax.broadcasted_iota(jnp.int32, (rows, n_dev), 1)
                for i, s in enumerate((q * 2 + c, q * 2 + 1 - c)):
                    w = jnp.where(chunk == s, wcol[...], 0.0)
                    wblk[q, rows * i:rows * (i + 1)] = jnp.sum(w, axis=1, keepdims=True)

            n = pl.multiple_of(kind * 256, 256)
            a = jnp.concatenate([held[q * 2 + c], held[q * 2 + 1 - c]], axis=0)
            g = jnp.dot(a, gate_v[:, pl.ds(n, 256)], preferred_element_type=F32)
            u = jnp.dot(a, up_v[:, pl.ds(n, 256)], preferred_element_type=F32)
            h = (g / (1.0 + jnp.exp(-g)) * u * wblk[q]).astype(BF16)
            hbuf[q, :, pl.ds(pl.multiple_of(c * units + n, 256), 256)] = h[:rows]
            hsend[q, :, pl.ds(n, 256)] = h[rows:]

            @on(UP_LAST)
            def _():
                h_copy(q).start()

        @on(DOWN)
        def _():
            h_arrive(q).wait_recv()
            h = hbuf[q]
            for n in range(0, width, 512):
                p = jnp.dot(h, down_v[:, n:n + 512], preferred_element_type=F32)
                held[sums(q), :, n:n + 512] = p.astype(BF16)

        @pl.when((kind > DOWN) & (kind < SEND_X))
        def _():
            @on(TOK_A)
            def _():
                a_y(q).wait_recv()

                @pl.when(a_goes_up(zz, r))
                def _():
                    a_up(q).start()

                @pl.when(a_goes_down(zz, r))
                def _():
                    a_down(q).start()

                @pl.when((r == 0) & a_crosses(zz))
                def _():
                    a_y(q).start()

                x_copy(q).start()

            @pl.when((kind == TOK_B0) | (kind == TOK_B1))
            def _():
                h = kind - TOK_B0
                b_y(q, h).wait_recv()
                forward_b(q, zz, h)
                b_y(q, h).start()

            @on(TOK_BO)
            def _():
                b_y(q, 0).wait_recv()
                b_y(q, 1).wait_recv()

            @pl.when((kind == TOK_B1) | (kind == TOK_BO))
            def _():
                core_copy(q, c).start()

            @on(TOK_X)
            def _():
                x_arrive(q).wait_recv()
                core_x_copy(q, c).start()

            @pl.when(kind >= OWN0)
            def _():
                forward_b(q, zz, kind - OWN0)

        @pl.when((kind >= SEND_X) & (kind < CHAIN_C))
        def _():
            @on(SEND_X)
            def _():
                sx_copy(q).start()

            @on(SEND_Y)
            def _():
                sy_copy(zz, q, 0).start()
                sy_copy(zz, q, 1).start()

            @on(SUM_X)
            def _():
                sx_copy(q).wait_recv()
                add(q, ra, keep, got_x[q])

            for i in range(2):
                @on(SUM_Y + i)
                def _():
                    sy_copy(zz, q, i).wait_recv()
                    add(q, rbs[i], slice(None), got_y[i, zz])
                    yx_copy(zz, q, i).start()

            for i in range(2):
                @on(SUM_YX + i)
                def _():
                    yx_copy(zz, q, i).wait_recv()
                    add(q, rbs[i], keep, got_yx[i, zz])

        def chain(i):
            got, _, _, part_rows = chains[i]

            @pl.when(((zz > z) & (z > 0)) | ((zz < z) & (z < 3)))
            def _():
                chain_arrive(i, zz, q).wait_recv()
                add(q, part_rows, keep, got[zz])

            @pl.when(zz > z)
            def _():
                chain_up(i, zz, q).start()

            @pl.when(zz < z)
            def _():
                chain_down(i, zz, q).start()

        def finish(i):
            got, _, _, part_rows = chains[i]

            @pl.when(z > 0)
            def _():
                chain_arrive(i, z, q).wait_recv()
                add(q, part_rows, keep, got[z])

            @pl.when(z < 3)
            def _():
                chain_arrive(i, 4, q).wait_recv()
                add(q, part_rows, keep, got[4])

        @pl.when(kind >= CHAIN_C)
        def _():
            @pl.when((kind == OTHER) & (zz == 0))
            def _():
                lax.fori_loop(1, n_dev, got_w, 0)
                expert = lax.broadcasted_iota(jnp.int32, (n_dev, experts, rows), 1)
                wcol[...] = jnp.sum(jnp.where(expert == e, wall[...], 0.0), axis=1).T
                load_gate.wait()
                load_up.wait()

            @pl.when((kind == OTHER) & (zz == 2))
            def _():
                lax.fori_loop(1, n_dev, drain_w, 0)
                down_copy(mine).wait_send()
                lax.fori_loop(0, 8, drain_tokens, 0)

            @pl.when((kind == OTHER) & (zz == 1))
            def _():
                load_down.wait()
                down_copy(theirs).wait_recv()

            for i, k in enumerate((CHAIN_C, CHAIN_O, CHAIN_B, CHAIN_B1)):
                @on(k)
                def _():
                    chain(i)

            @on(END_O)
            def _():
                finish(1)
                end_copy(q).start()

            @on(END_C)
            def _():
                finish(0)
                end_copy(q).wait_recv()
                add(q, ra, keep, got_end[...])
                out[ra] = held[sums(q), ra, keep]

            for i in range(2):
                @on(END_B + i)
                def _():
                    finish(2 + i)
                    out[rbs[i]] = held[sums(q), rbs[i], keep]

    def steps(i, carry):
        word = word_at(z, i)

        def one(k, rest):
            run(rest % BASE)
            return rest // BASE

        lax.fori_loop(0, 4, one, word)
        return carry

    lax.fori_loop(0, len(WORDS[0]), steps, 0)

    def drain(q, carry):
        zz = q // 2
        own_row = q % 2 == y

        sx_copy(q).wait_send()

        @pl.when(own_row)
        def _():
            yx_copy(zz, q, 0).wait_send()
            yx_copy(zz, q, 1).wait_send()

        @pl.when(~own_row)
        def _():
            sy_copy(zz, q, 0).wait_send()
            sy_copy(zz, q, 1).wait_send()

        for i in range(4):
            @pl.when((own_row if i != 1 else ~own_row) & (zz > z))
            def _():
                chain_up(i, zz, q).wait_send()

            @pl.when((own_row if i != 1 else ~own_row) & (zz < z))
            def _():
                chain_down(i, zz, q).wait_send()

        return carry

    lax.fori_loop(0, 8, drain, 0)
    end_copy(z * 2 + 1 - y).wait_send()


def dense_weights(expert_ids, route_weights, experts):
    hit = expert_ids[None] == jnp.arange(experts, dtype=jnp.int32)[:, None, None]
    return jnp.sum(jnp.where(hit, route_weights[None], 0.0), axis=2)


def on_box(tokens, expert_ids, route_weights, gate_w, up_w, down_w):
    rows, width = tokens.shape
    n_dev = lax.axis_size("expert")
    units = gate_w.shape[2]
    any_ = pl.BlockSpec(memory_space=pl.ANY)
    vmem = pl.BlockSpec(memory_space=pltpu.VMEM)
    sem = lambda *s: pltpu.SemaphoreType.DMA(s)
    buf = lambda *s: pltpu.VMEM(s, BF16)
    half = width // 2
    top = TOP
    low = rows - top
    return pl.pallas_call(
        layer_kernel,
        out_shape=jax.ShapeDtypeStruct((rows, half), BF16),
        in_specs=[any_] * 6,
        out_specs=vmem,
        scratch_shapes=[
            buf(n_dev, rows, width), buf(width, units), buf(width, units), buf(2 * units, width),
            pltpu.VMEM((n_dev, n_dev, rows), F32), pltpu.VMEM((rows, n_dev), F32),
            pltpu.VMEM((8, 2 * rows, 1), F32), pltpu.VMEM(expert_ids.shape[::-1], jnp.int32),
            pltpu.VMEM(route_weights.shape[::-1], F32),
            buf(8, rows, 2 * units), buf(8, rows, units),
            buf(8, top, half), buf(2, 4, low // 2, width), buf(2, 4, low // 2, half),
            buf(5, top, half), buf(5, top, half), buf(5, low // 2, half), buf(5, low // 2, half), buf(top, half),
            sem(6), sem(n_dev), sem(n_dev), sem(2, 8), sem(2, 4, 2), sem(4), sem(4, 2), sem(8),
            sem(8), sem(8), sem(8), sem(1),
            sem(8), sem(8, 2), sem(8), sem(8), sem(8), sem(8), sem(1),
            sem(8), sem(8), sem(2, 4), sem(2, 4), sem(2, 4), sem(2, 4),
            sem(4), sem(5), sem(4), sem(5), sem(4), sem(5), sem(4), sem(5), sem(1), sem(1),
        ],
        compiler_params=pltpu.CompilerParams(
            collective_id=0, has_side_effects=True, vmem_limit_bytes=62 * 2**20
        ),
        name="moe_layer",
    )(tokens, expert_ids.T, route_weights.T, gate_w, up_w, down_w)


def anywhere(tokens, expert_ids, route_weights, gate_w, up_w, down_w):
    rows, width = tokens.shape
    local_experts = gate_w.shape[0]
    experts = local_experts * lax.axis_size("expert")
    first = lax.axis_index("expert") * local_experts
    wts = dense_weights(expert_ids, route_weights, experts)
    every = lax.all_gather(tokens, "expert", axis=0, tiled=True)
    wall = lax.all_gather(wts, "expert", axis=1, tiled=True)
    total = None
    for i in range(local_experts):
        w = lax.dynamic_index_in_dim(wall, first + i, 0, keepdims=False)[:, None]
        g = jnp.dot(every, gate_w[i], preferred_element_type=F32)
        u = jnp.dot(every, up_w[i], preferred_element_type=F32)
        h = (jax.nn.silu(g) * u * w).astype(BF16)
        p = jnp.dot(h, down_w[i], preferred_element_type=F32)
        total = p if total is None else total + p
    mixed = lax.psum_scatter(total.astype(BF16), "expert", scatter_dimension=0, tiled=True)
    return lax.psum_scatter(mixed, "tensor", scatter_dimension=1, tiled=True)


def solution(mesh):
    shape = dict(mesh.shape)
    box = shape == {"groups": 1, "expert": 16, "tensor": 2}
    in_specs = (
        P(("groups", "expert"), None),
        P(("groups", "expert"), None),
        P(("groups", "expert"), None),
        P("expert", None, "tensor"),
        P("expert", None, "tensor"),
        P("expert", "tensor", None),
    )
    out_specs = P(("groups", "expert"), "tensor")
    return jax.shard_map(
        on_box if box else anywhere, mesh=mesh, in_specs=in_specs, out_specs=out_specs, check_vma=False
    )
```
